32 devices in a mesh: win: 2 (over y), rows: 4 (over z), cols: 4 (over x, core).
Axes of the slice: x: 2, y: 2, z: 4, core: 2. Of those that a mesh axis runs over, the one named last changes fastest.
Arguments:
- feat_one: bfloat16 [256, 128, 48], P(('win', 'rows'), 'cols'), parts along dimension 0, may hold values from -6 to 6
- feat_two: bfloat16 [128, 64, 96], P(('win', 'rows'), 'cols'), parts along dimension 0, may hold values from -6 to 6
- feat_three: bfloat16 [64, 32, 192], P(('win', 'rows'), 'cols'), parts along dimension 0, may hold values from -6 to 6
- feat_four: bfloat16 [32, 16, 384], P(('win', 'rows'), 'cols'), parts along dimension 0, may hold values from -6 to 6
- conv_one: bfloat16 [864, 48], P(None, 'cols'), may hold values from -0.3125 to 0.3125
- conv_two: bfloat16 [1728, 96], P(None, 'cols'), may hold values from -0.21875 to 0.21875
- conv_three: bfloat16 [3456, 192], P(None, 'cols'), may hold values from -0.15625 to 0.15625
- conv_four: bfloat16 [6912, 384], P(None, 'cols'), may hold values from -0.109375 to 0.109375
- down_one: bfloat16 [432, 816], P(None, 'cols'), may hold values from -0.3125 to 0.3125
- down_two: bfloat16 [864, 672], P(None, 'cols'), may hold values from -0.21875 to 0.21875
- down_three: bfloat16 [1728, 384], P(None, 'cols'), may hold values from -0.15625 to 0.15625
- lift_two: bfloat16 [96, 48], P(None, 'cols'), may hold values from -0.625 to 0.625
- lift_three: bfloat16 [192, 144], P(None, 'cols'), may hold values from -0.4375 to 0.4375
- lift_four: bfloat16 [384, 336], P(None, 'cols'), may hold values from -0.3125 to 0.3125
- biases: float32 [3840], replicated, may hold values from -3 to 3
Outputs:
- joined_one: bfloat16 [256, 128, 48], P(('win', 'rows'), 'cols'), parts along dimension 0
- joined_two: bfloat16 [128, 64, 96], P(('win', 'rows'), 'cols'), parts along dimension 0
- joined_three: bfloat16 [64, 32, 192], P(('win', 'rows'), 'cols'), parts along dimension 0
- joined_four: bfloat16 [32, 16, 384], P(('win', 'rows'), 'cols'), parts along dimension 0
The draws below stay inside these ranges and needn't reach their ends.
There are 2 independent parts, one for each index of `win`. The reference program is written for one: setup_inputs(seed, part) draws one part's arguments, and reference() takes and returns one part's arrays. A program takes and returns all parts, laid end to end along the dimension named above; an argument that names none is the same for every part. Nothing has to cross between parts.
All inputs are finite; a program needn't handle non-finite values.
Results may differ from the reference program's by a relative error of at most 0.0055.
Values may be sent and summed in bfloat16 or wider, within the bound.
No kernel may reach another device: no remote copies, remote signals or barrier semaphores. Data moves between devices by JAX's collectives and lax.ppermute only.
A program may use at most 64 MiB of HBM per device.

```python
import jax
import jax.numpy as jnp
from jax import lax

C1 = 48
C2 = 96
C3 = 192
C4 = 384
BLOCKS = 1
H1 = 128
W1 = 128
H2 = 64
W2 = 64
H3 = 32
W3 = 32
H4 = 16
W4 = 16


def levels(rng, dims, shards, low, high):
    def one(axis_at, shards_of):
        draws = jax.random.uniform(jax.random.fold_in(jax.random.fold_in(rng, 6), axis_at), (shards_of,), jnp.float32, low / len(shards), high / len(shards))
        return jnp.repeat(jnp.exp(draws), dims[axis_at] // shards_of).reshape((-1,) + (1,) * (len(dims) - axis_at - 1))

    factor_of = one(*shards[0])
    for cut in shards[1:]:
        factor_of = factor_of * one(*cut)
    return factor_of


def noise(rng, dims, spread, limit, split=(), dtype=jnp.bfloat16):
    array = jax.random.normal(rng, dims, jnp.float32) * spread
    if len(split) > 0:
        array = levels(rng, dims, split, -0.22, 0.18) * array
    return jnp.clip(array, min=-limit, max=limit).astype(dtype)


def setup_inputs(seed: int = 0, part: int = 0) -> dict:
    seeds = jax.random.split(jax.random.key(seed), 16)
    own_keys = jax.random.split(jax.random.fold_in(seeds[15], part), 16)
    feat_one = noise(own_keys[0], (H1, W1, C1), 1.0, 6.0, ((0, 4), (1, 4)))
    feat_two = noise(own_keys[1], (H2, W2, C2), 1.0, 6.0, ((0, 4), (1, 4)))
    feat_three = noise(own_keys[2], (H3, W3, C3), 1.0, 6.0, ((0, 4), (1, 4)))
    feat_four = noise(own_keys[3], (H4, W4, C4), 1.0, 6.0, ((0, 4), (1, 4)))
    conv_one = noise(seeds[4], (18 * BLOCKS * C1, C1), (9 * C1) ** -0.5, 0.3125, ((1, 4),))
    conv_two = noise(seeds[5], (18 * BLOCKS * C2, C2), (9 * C2) ** -0.5, 0.21875, ((1, 4),))
    conv_three = noise(seeds[6], (18 * BLOCKS * C3, C3), (9 * C3) ** -0.5, 0.15625, ((1, 4),))
    conv_four = noise(seeds[7], (18 * BLOCKS * C4, C4), (9 * C4) ** -0.5, 0.109375, ((1, 4),))
    down_one = noise(seeds[8], (9 * C1, 17 * C1), (9 * C1) ** -0.5, 0.3125, ((1, 4),))
    down_two = noise(seeds[9], (9 * C2, 14 * C1), (9 * C2) ** -0.5, 0.21875, ((1, 4),))
    down_three = noise(seeds[10], (9 * C3, C4), (9 * C3) ** -0.5, 0.15625, ((1, 4),))
    lift_two = noise(seeds[11], (C2, C1), C2 ** -0.5, 0.625, ((1, 4),))
    lift_three = noise(seeds[12], (C3, 3 * C1), C3 ** -0.5, 0.4375, ((1, 4),))
    lift_four = noise(seeds[13], (C4, 7 * C1), C4 ** -0.5, 0.3125, ((1, 4),))
    biases = noise(seeds[14], ((30 * BLOCKS + 50) * C1,), 0.5, 3.0, (), jnp.float32)
    return {"feat_one": feat_one, "feat_two": feat_two, "feat_three": feat_three, "feat_four": feat_four, "conv_one": conv_one, "conv_two": conv_two, "conv_three": conv_three, "conv_four": conv_four, "down_one": down_one, "down_two": down_two, "down_three": down_three, "lift_two": lift_two, "lift_three": lift_three, "lift_four": lift_four, "biases": biases}


def offsets(width, blocks):
    start = 30 * blocks * width
    return (start, start + 17 * width, start + 31 * width, start + 39 * width, start + 40 * width, start + 43 * width)


def conv_full(inputs, weight, bias, stride):
    inputs = lax.optimization_barrier(inputs)
    channels = inputs.shape[-1]
    kernel = weight.astype(jnp.float32).reshape(3, 3, channels, weight.shape[1])
    result = lax.conv_general_dilated(inputs.astype(jnp.float32)[None], kernel, (stride, stride), ((1, 1), (1, 1)), dimension_numbers=("NHWC", "HWIO", "NHWC"), precision=lax.Precision.HIGHEST)
    return result[0] + bias


def enlarge(values, factor):
    return jnp.repeat(jnp.repeat(values, factor, axis=0), factor, axis=1)


def branch_blocks(feat, weight, biases, level, base_width):
    width = feat.shape[-1]
    base = 2 * BLOCKS * base_width * (2 ** level - 1)
    for block in range(BLOCKS):
        first = weight[(2 * block) * 9 * width:(2 * block + 1) * 9 * width]
        second = weight[(2 * block + 1) * 9 * width:(2 * block + 2) * 9 * width]
        bias_a = biases[base + 2 * block * width:base + (2 * block + 1) * width]
        bias_b = biases[base + (2 * block + 1) * width:base + (2 * block + 2) * width]
        middle = jax.nn.relu(conv_full(feat, first, bias_a, 1)).astype(jnp.bfloat16)
        feat = jax.nn.relu(conv_full(middle, second, bias_b, 1) + feat.astype(jnp.float32)).astype(jnp.bfloat16)
    return feat


def point_conv(feat, weight, bias):
    height, breadth, channels = feat.shape
    flat = jnp.dot(feat.reshape(height * breadth, channels), weight, preferred_element_type=jnp.float32)
    return flat.reshape(height, breadth, weight.shape[1]) + bias


def reference(feat_one, feat_two, feat_three, feat_four, conv_one, conv_two, conv_three, conv_four, down_one, down_two, down_three, lift_two, lift_three, lift_four, biases):
    unit = feat_one.shape[-1]
    y_one = branch_blocks(feat_one, conv_one, biases, 0, unit)
    y_two = branch_blocks(feat_two, conv_two, biases, 1, unit)
    y_three = branch_blocks(feat_three, conv_three, biases, 2, unit)
    y_four = branch_blocks(feat_four, conv_four, biases, 3, unit)
    off_d1, off_d2, off_d3, off_l2, off_l3, off_l4 = offsets(unit, BLOCKS)

    def down_group(feat, weight, base, start, stop):
        return conv_full(feat, weight[:, start:stop], biases[base + start:base + stop], 2)

    d12 = down_group(y_one, down_one, off_d1, 0, 2 * unit)
    t13 = jax.nn.relu(down_group(y_one, down_one, off_d1, 2 * unit, 3 * unit)).astype(jnp.bfloat16)
    t14 = jax.nn.relu(down_group(y_one, down_one, off_d1, 3 * unit, 4 * unit)).astype(jnp.bfloat16)
    d13 = down_group(t13, down_one, off_d1, 4 * unit, 8 * unit)
    t14b = jax.nn.relu(down_group(t14, down_one, off_d1, 8 * unit, 9 * unit)).astype(jnp.bfloat16)
    d14 = down_group(t14b, down_one, off_d1, 9 * unit, 17 * unit)
    d23 = down_group(y_two, down_two, off_d2, 0, 4 * unit)
    t24 = jax.nn.relu(down_group(y_two, down_two, off_d2, 4 * unit, 6 * unit)).astype(jnp.bfloat16)
    d24 = down_group(t24, down_two, off_d2, 6 * unit, 14 * unit)
    d34 = conv_full(y_three, down_three, biases[off_d3:off_d3 + 8 * unit], 2)
    u_two = point_conv(y_two, lift_two, biases[off_l2:off_l2 + unit])
    u_three = point_conv(y_three, lift_three, biases[off_l3:off_l3 + 3 * unit])
    u_four = point_conv(y_four, lift_four, biases[off_l4:off_l4 + 7 * unit])
    joined_one = y_one.astype(jnp.float32) + enlarge(u_two, 2) + enlarge(u_three[:, :, :unit], 4) + enlarge(u_four[:, :, :unit], 8)
    joined_two = d12 + y_two.astype(jnp.float32) + enlarge(u_three[:, :, unit:], 2) + enlarge(u_four[:, :, unit:3 * unit], 4)
    joined_three = d13 + d23 + y_three.astype(jnp.float32) + enlarge(u_four[:, :, 3 * unit:], 2)
    joined_four = d14 + d24 + d34 + y_four.astype(jnp.float32)
    return (jax.nn.relu(joined_one).astype(jnp.bfloat16), jax.nn.relu(joined_two).astype(jnp.bfloat16), jax.nn.relu(joined_three).astype(jnp.bfloat16), jax.nn.relu(joined_four).astype(jnp.bfloat16))
```

```python
import functools

import jax
import jax.numpy as jnp
from jax import lax
from jax.experimental import pallas as pl
from jax.experimental.pallas import tpu as pltpu
from jax.sharding import PartitionSpec as P

F32 = jnp.float32
BF16 = jnp.bfloat16
LANES = 128
BEFORE = (9, 5, 3, 2)
AFTER = 2


def up_to(value, multiple):
    return -(-value // multiple) * multiple


def dot(a, b):
    return jnp.dot(a.astype(BF16), b.astype(BF16), preferred_element_type=F32)


def iota(shape, dim):
    return lax.broadcasted_iota(jnp.int32, shape, dim)


def onehot(condition):
    return jnp.where(condition, 1.0, 0.0).astype(F32).astype(BF16)


def taps(ref, height, breadth, stride, row, col, weight_of, lanes=None):
    total = None
    for r in range(3):
        for q in range(3):
            rows = pl.ds(row + r, height, stride=stride) if stride > 1 else pl.ds(row + r, height)
            cols = pl.ds(col + q, breadth, stride=stride) if stride > 1 else pl.ds(col + q, breadth)
            if stride > 1:
                block = wide_load(ref, rows, cols)[:, :, lanes[0] : lanes[1]]
            else:
                block = ref[rows, cols, :]
            flat = block.reshape(height * breadth, block.shape[2])
            part = dot(flat, weight_of(3 * r + q))
            total = part if total is None else total + part
    return total


def wide_load(refs, rows, cols):
    parts = [ref[rows, cols, :] for ref in refs]
    return parts[0] if len(parts) == 1 else jnp.concatenate(parts, axis=2)


def wide_store(refs, rows, cols, value):
    channels = value.shape[2]
    for i, ref in enumerate(refs):
        part = value[:, :, i * LANES : min((i + 1) * LANES, channels)]
        if part.shape[2] < LANES:
            rest = jnp.zeros(part.shape[:2] + (LANES - part.shape[2],), part.dtype)
            part = jnp.concatenate([part, rest], axis=2)
        ref[rows, cols, :] = part


def inside(shape, row_first, row_count, col_first, col_count):
    rows = iota(shape, 0) + row_first
    cols = iota(shape, 1) + col_first
    return (rows >= 0) & (rows < row_count) & (cols >= 0) & (cols < col_count)


def rounded(value):
    return value.astype(BF16).astype(F32)


def vmem(count):
    return [pl.BlockSpec(memory_space=pltpu.VMEM)] * count


PARAMS = pltpu.CompilerParams(vmem_limit_bytes=56 * 1024 * 1024)


class RowLayout:
    def __init__(self, shapes, counts):
        self.counts = counts
        self.half = shapes[0][1] // 2
        self.start = []
        at = 0
        for level, ((_, breadth, channels), count) in enumerate(zip(shapes, counts)):
            self.start.append(at)
            positions = count * (self.half if level == 0 else breadth)
            at += positions * (1 if level == 0 else -(-channels // LANES))
        self.total = up_to(at, 16)


def pack_rows(layout, refs, firsts, scratch):
    one, two, three, four = refs
    count = layout.counts
    half = layout.half
    for part in range(2):
        block = one[firsts[0] : firsts[0] + count[0], part * half : (part + 1) * half, :]
        size = count[0] * half
        scratch[0:size, part * 64 : part * 64 + one.shape[2]] = block.astype(F32).reshape(size, -1)
    at = layout.start[1]
    size = count[1] * two.shape[1]
    block = two[firsts[1] : firsts[1] + count[1], :, :].astype(F32).reshape(size, two.shape[2])
    scratch[at : at + size, 0 : two.shape[2]] = block
    at = layout.start[2]
    size = count[2] * three.shape[1]
    block = three[firsts[2] : firsts[2] + count[2], :, :].astype(F32).reshape(size, three.shape[2])
    for low in range(0, three.shape[2], LANES):
        high = min(low + LANES, three.shape[2])
        scratch[at : at + size, 0 : high - low] = block[:, low:high]
        at += size
    breadth = four.shape[1]
    size = count[3] * breadth
    for row in range(count[3]):
        block = four[firsts[3] + row].astype(F32)
        at = layout.start[3] + row * breadth
        for low in range(0, four.shape[2], LANES):
            scratch[at : at + breadth, 0:LANES] = block[:, low : low + LANES]
            at += size


def rows_kernel(layouts, one, two, three, four, down_ref, up_ref, scratch):
    refs = (one, two, three, four)
    low, high = layouts
    firsts = tuple(ref.shape[0] - count for ref, count in zip(refs, low.counts))
    scratch[...] = jnp.zeros_like(scratch)
    pack_rows(low, refs, firsts, scratch)
    down_ref[...] = scratch[0 : low.total, :].astype(BF16)
    pack_rows(high, refs, (0, 0, 0, 0), scratch)
    up_ref[...] = scratch[0 : high.total, :].astype(BF16)


def stretch_fine(level, layout_pair, feat, top, bottom, target, col):
    low, high = layout_pair
    height, breadth, channels = feat.shape
    before, after = low.counts[level], high.counts[level]
    for layout, message, row, count in (
        (low, top, 0, before),
        (high, bottom, before + height, after),
    ):
        at = layout.start[level]
        if level == 0:
            half = layout.half
            for part in range(2):
                block = message[at : at + count * half, part * 64 : part * 64 + channels]
                target[row : row + count, col + part * half : col + (part + 1) * half, :] = (
                    block.astype(F32).reshape(count, half, channels)
                )
        else:
            block = message[at : at + count * breadth, 0:channels]
            target[row : row + count, col : col + breadth, :] = block.astype(F32).reshape(
                count, breadth, channels
            )
    target[before : before + height, col : col + breadth, :] = feat[...].astype(F32)


def columns_kernel(layouts, one, two, three, four, top, bottom, gather_ref, right_ref, left_ref,
                   full_one, full_two, full_three, message, edge):
    low, high = layouts
    breadth, channels = three.shape[1], three.shape[2]
    own = three.shape[0] * breadth
    before, after = low.counts[2] * breadth, high.counts[2] * breadth
    for layout, source, row, size in ((low, top, 0, before), (high, bottom, before + own, after)):
        at = layout.start[2]
        for first in range(0, channels, LANES):
            last = min(first + LANES, channels)
            full_three[row : row + size, first:last] = source[at : at + size, 0 : last - first].astype(F32)
            at += size
    full_three[before : before + own, :] = three[...].astype(F32).reshape(own, channels)
    size_four = gather_four(four.shape)
    breadth, channels4 = four.shape[1], four.shape[2]
    before, after = low.counts[3] * breadth, high.counts[3] * breadth
    for layout, source, row, size in (
        (low, top, 0, before),
        (high, bottom, before + four.shape[0] * breadth, after),
    ):
        at = layout.start[3]
        for first in range(0, channels4, LANES):
            message[row : row + size, first : first + LANES] = source[at : at + size, :].astype(F32)
            at += size
    for row in range(four.shape[0]):
        at = before + row * breadth
        message[at : at + breadth, 0:channels4] = four[row].astype(F32)
    total, head = gather_three(three.shape)
    message[size_four : size_four + head, 0:channels] = full_three[0:head, :]
    message[size_four : size_four + total - head, channels : 2 * channels] = full_three[head:total, :]
    gather_ref[...] = message[...].astype(BF16)
    stretch_fine(0, layouts, one, top, bottom, full_one, 0)
    stretch_fine(1, layouts, two, top, bottom, full_two, 0)
    wide, wide_two = one.shape[1], two.shape[1]
    left, left_two = BEFORE[0], BEFORE[1]
    rows, rows_two = full_one.shape[0], full_two.shape[0]
    edge[:, 0:left, 0 : one.shape[2]] = full_one[:, wide - left : wide, :]
    edge[0:rows_two, left : left + left_two, 0 : two.shape[2]] = full_two[
        :, wide_two - left_two : wide_two, :
    ]
    right_ref[...] = edge[...].astype(BF16)
    edge[:, 0:AFTER, 0 : one.shape[2]] = full_one[:, 0:AFTER, :]
    edge[0:rows_two, AFTER : 2 * AFTER, 0 : two.shape[2]] = full_two[:, 0:AFTER, :]
    left_ref[...] = edge[:, 0:8, :].astype(BF16)


def gather_four(shape):
    return (shape[0] + BEFORE[3] + AFTER) * shape[1]


def gather_three(shape):
    total = (shape[0] + BEFORE[2] + AFTER) * shape[1]
    return total, up_to(-(-total // 2), 8)


def own_channels(me, channels, own):
    return onehot(iota((channels, own), 0) == iota((channels, own), 1) + me * own)


def own_bias(bias_ref, first, channels, me, own):
    row = jnp.broadcast_to(bias_ref[0:1, first : first + channels], (8, channels))
    pick = jnp.where(iota((channels, own), 0) == iota((channels, own), 1) + me * own, 1.0, 0.0)
    return jnp.dot(row, pick.astype(F32), precision=lax.Precision.HIGHEST, preferred_element_type=F32)[0:1]


def spread(target, blocks, me, rows, block_cols):
    shift = block_cols.bit_length() - 1
    width = target.shape[1]
    total = None
    for k, block in enumerate(blocks):
        size = block.shape[0]
        shape = (rows, width, size)
        source = iota(shape, 2)
        slot = (me ^ k) * block_cols + 1 + (source & (block_cols - 1))
        choose = ((source >> shift) == iota(shape, 0)) & (iota(shape, 1) == slot)
        part = dot(onehot(choose).reshape(rows * width, size), block)
        total = part if total is None else total + part
    target[...] = total.reshape(rows, width, total.shape[1])


def coarse_first_kernel(sizes, index, *refs):
    count, high3, wide3, chan3, high4, wide4, chan4, bias3, bias4 = sizes
    blocks = refs[:count]
    conv3, conv4, bias, out, res3, res4, full3, full4, message = refs[count:]
    row, me = index[0], index[1]
    size4 = gather_four((high4, wide4))
    total3, head = gather_three((high3, wide3))
    spread(full4, [b[0:size4, 0:chan4] for b in blocks], me, high4 + BEFORE[3] + AFTER, wide4)
    parts = []
    for b in blocks:
        parts.append(
            jnp.concatenate(
                [
                    b[size4 : size4 + head, 0:chan3].astype(F32),
                    b[size4 : size4 + total3 - head, chan3 : 2 * chan3].astype(F32),
                ],
                axis=0,
            )
        )
    spread(full3, parts, me, high3 + BEFORE[2] + AFTER, wide3)
    heights = []
    for full, conv, high, wide, chan, before, base in (
        (full3, conv3, high3, wide3, chan3, BEFORE[2], bias3),
        (full4, conv4, high4, wide4, chan4, BEFORE[3], bias4),
    ):
        own = chan // count
        out_high = high + before + AFTER - 2
        out_wide = wide * count
        mid = taps(full, out_high, out_wide, 1, 0, 0, lambda t: conv[t * chan : (t + 1) * chan, :])
        mid = jax.nn.relu(mid + own_bias(bias, base, chan, me, own)).reshape(out_high, out_wide, own)
        rows = iota(mid.shape, 0) + row * high - (before - 1)
        valid = (rows >= 0) & (rows < index[2] * high)
        heights.append(jnp.where(valid, mid, 0.0).reshape(out_high * out_wide, own))
    mid3, mid4 = heights
    half = mid3.shape[0] // 2
    own3, own4 = mid3.shape[1], mid4.shape[1]
    message[0:half, 0:own3] = mid3[0:half]
    message[0:half, 64 : 64 + own3] = mid3[half:]
    message[half : half + mid4.shape[0], 0:own4] = mid4
    out[...] = message[...].astype(BF16)
    skip3 = BEFORE[2] - 1
    keep = full3[skip3 : skip3 + high3 + 1, 1 : 1 + wide3 * count, :].reshape(-1, chan3)
    res3[...] = dot(keep, own_channels(me, chan3, own3)).astype(BF16)
    keep = full4[BEFORE[3] : BEFORE[3] + high4, 1 : 1 + wide4 * count, :].reshape(-1, chan4)
    res4[...] = dot(keep, own_channels(me, chan4, own4)).astype(BF16)


def natural(blocks, me, own, channels):
    total = None
    for k, block in enumerate(blocks):
        place = onehot(iota((own, channels), 1) == iota((own, channels), 0) + (me ^ k) * own)
        part = dot(block, place)
        total = part if total is None else total + part
    return total


def message_rows(sizes):
    count, high3, wide3, chan3, high4, wide4, chan4, _, _ = sizes
    half = (high3 + BEFORE[2] + AFTER - 2) * wide3 * count // 2
    return half, half + (high4 + BEFORE[3] + AFTER - 2) * wide4 * count


def coarse_second_kernel(sizes, index, *refs):
    count, high3, wide3, chan3, high4, wide4, chan4, bias3, bias4 = sizes
    blocks = refs[:count]
    res3, res4, conv3, conv4, bias = refs[count : count + 5]
    outs = refs[count + 5 : 2 * count + 5]
    full3, full4, message = refs[2 * count + 5 :]
    row, me = index[0], index[1]
    own3, own4 = chan3 // count, chan4 // count
    half, last = message_rows(sizes)
    mids3 = [
        jnp.concatenate([b[0:half, 0:own3].astype(F32), b[0:half, 64 : 64 + own3].astype(F32)], axis=0)
        for b in blocks
    ]
    mids4 = [b[half:last, 0:own4] for b in blocks]
    results = []
    for full, mids, conv, res, high, wide, chan, before, base, extra in (
        (full3, mids3, conv3, res3, high3, wide3, chan3, BEFORE[2], bias3, 1),
        (full4, mids4, conv4, res4, high4, wide4, chan4, BEFORE[3], bias4, 0),
    ):
        own = chan // count
        mid_high = high + before + AFTER - 2
        out_wide = wide * count
        full[...] = jnp.zeros_like(full)
        full[:, 1 : 1 + out_wide, :] = natural(mids, me, own, chan).reshape(mid_high, out_wide, chan)
        out_high = high + extra
        first = 9 * chan
        y = taps(
            full, out_high, out_wide, 1, 0, 0,
            lambda t: conv[first + t * chan : first + (t + 1) * chan, :],
        )
        y = y + own_bias(bias, base + chan, chan, me, own) + res[...].astype(F32)
        y = jax.nn.relu(y).reshape(out_high, out_wide, own)
        rows = iota(y.shape, 0) + row * high - extra
        y = jnp.where((rows >= 0) & (rows < index[2] * high), y, 0.0)
        results.append(y.reshape(out_high * out_wide, own))
    y3, y4 = results
    for k, out in enumerate(outs):
        target = me ^ k
        wide = wide3 * count
        shape = (high3 + 1, 16, y3.shape[0])
        source = iota(shape, 2)
        slot = iota(shape, 1)
        choose = (
            ((source >> (wide.bit_length() - 1)) == iota(shape, 0))
            & ((source & (wide - 1)) == target * wide3 - 1 + slot)
            & (slot < wide3 + 1)
        )
        part = dot(onehot(choose).reshape((high3 + 1) * 16, -1), y3)
        cut = part.shape[0] // 2
        message[0:cut, 0:own3] = part[0:cut]
        message[0:cut, 64 : 64 + own3] = part[cut:]
        wide = wide4 * count
        shape = (high4, 8, y4.shape[0])
        source = iota(shape, 2)
        slot = iota(shape, 1)
        choose = (
            ((source >> (wide.bit_length() - 1)) == iota(shape, 0))
            & ((source & (wide - 1)) == target * wide4 + slot)
            & (slot < wide4)
        )
        part = dot(onehot(choose).reshape(high4 * 8, -1), y4)
        message[cut : cut + high4 * 8, 0:own4] = part
        out[...] = message[...].astype(BF16)


class Packing:
    def __init__(self, shapes):
        items = []
        for name, (rows, width) in shapes.items():
            for low in range(0, width, LANES):
                items.append((rows, min(LANES, width - low), name, low))
        items.sort(key=lambda item: (-item[0], -item[1], item[2]))
        blocks = []
        self.pieces = []
        for rows, width, name, low in items:
            for block in blocks:
                if block[1] + width <= LANES:
                    break
            else:
                block = [rows, 0, sum(b[0] for b in blocks)]
                blocks.append(block)
            self.pieces.append((name, low, width, rows, block[2], block[1]))
            block[1] += width
        self.total = sum(b[0] for b in blocks)

    def ranges(self, names):
        spans = sorted({(p[4], p[4] + p[3]) for p in self.pieces if p[0] in names})
        merged = []
        for low, high in spans:
            if merged and low <= merged[-1][1]:
                merged[-1][1] = max(merged[-1][1], high)
            else:
                merged.append([low, high])
        return merged

    def assemble(self, name, stacked, width, groups, target):
        count = stacked.shape[0]
        starts = aligned(groups)
        for piece, low, size, rows, row, lane in self.pieces:
            if piece != name:
                continue
            for j in range(count):
                at = j * width + low
                end = at + size
                first = 0
                for group, start in zip(groups, starts):
                    a, b = max(at, first), min(end, first + group)
                    if a < b:
                        target[0:rows, start + a - first : start + b - first] = stacked[
                            j, row : row + rows, lane + a - at : lane + b - at
                        ]
                    first += group


def aligned(groups):
    starts, at = [], 0
    for group in groups:
        starts.append(at)
        at += up_to(group, LANES)
    return starts


def aligned_width(groups):
    return sum(up_to(group, LANES) for group in groups)


def pack_kernel(packing, names, *refs):
    sources = dict(zip(names, refs[:-1]))
    out = refs[-1]
    for name, low, size, rows, row, lane in packing.pieces:
        out[row : row + rows, lane : lane + size] = sources[name][:, low : low + size]


def fetch(packing, names, me, buffers, stacked, semaphores):
    copies = []
    for k, buffer in enumerate(buffers):
        for s, (low, high) in enumerate(packing.ranges(names)):
            copy = pltpu.make_async_copy(
                buffer.at[pl.ds(low, high - low)],
                stacked.at[me ^ k, pl.ds(low, high - low)],
                semaphores.at[k, s],
            )
            copy.start()
            copies.append(copy)
    return copies


def fine_kernel(plan, index, *refs):
    packing, layouts, count, unit, offs, widths = plan
    one, two, top, bottom, from_left, from_right, bias = refs[:7]
    buffers = refs[7 : 7 + count]
    y1_ref, y2_ref, d12_ref, d3_ref, d4_ref = refs[7 + count : 12 + count]
    (x1, m1, v1, t1, tb, s12, x2, m2, v2, t2, s3, k1, k2, g1, g2, stacked, semaphores) = refs[12 + count :]
    row, me, row_count, col_count = index[0], index[1], index[2], index[3]
    copies = fetch(packing, FINE, me, buffers, stacked, semaphores)
    high1, wide1, chan1 = one.shape
    high2, wide2, chan2 = two.shape
    stretch_fine(0, layouts, one, top, bottom, x1, 16)
    stretch_fine(1, layouts, two, top, bottom, x2, 16)
    b1, b2 = BEFORE[0], BEFORE[1]
    rows2 = high2 + b2 + AFTER
    x1[:, 16 - b1 : 16, :] = from_left[:, 0:b1, 0:chan1].astype(F32)
    x1[:, 16 + wide1 : 16 + wide1 + AFTER, :] = from_right[:, 0:AFTER, 0:chan1].astype(F32)
    x2[:, 16 - b2 : 16, :] = from_left[0:rows2, b1 : b1 + b2, 0:chan2].astype(F32)
    x2[:, 16 + wide2 : 16 + wide2 + AFTER, :] = from_right[
        0:rows2, AFTER : 2 * AFTER, 0:chan2
    ].astype(F32)
    for copy in copies:
        copy.wait()
    packing.assemble("conv_one", stacked, widths["conv_one"], (chan1,), k1)
    packing.assemble("conv_two", stacked, widths["conv_two"], (chan2,), k2)
    packing.assemble("down_one", stacked, widths["down_one"], groups_one(unit), g1)
    packing.assemble("down_two", stacked, widths["down_two"], groups_two(unit), g2)
    ys = []
    for x, m, v, k, before, high, wide, chan, base in (
        (x1, m1, v1, k1, b1, high1, wide1, chan1, 0),
        (x2, m2, v2, k2, b2, high2, wide2, chan2, 2 * unit),
    ):
        mid_high = high + before
        mid_wide = up_to(wide + before, 8)
        mid = taps(x, mid_high, mid_wide, 1, 0, 16 - before, lambda t: k[t * chan : (t + 1) * chan, 0:chan])
        mid = jax.nn.relu(mid + bias[0:1, base : base + chan]).reshape(mid_high, mid_wide, chan)
        ok = inside(
            mid.shape, row * high - before + 1, row_count * high, me * wide - before + 1, col_count * wide
        )
        m[:, 0:mid_wide, :] = rounded(jnp.where(ok, mid, 0.0))
        y_high = high + before - 2
        y_wide = up_to(wide + before - 2, 8)
        first = 9 * chan
        y = taps(
            m, y_high, y_wide, 1, 0, 0,
            lambda t: k[first + t * chan : first + (t + 1) * chan, 0:chan],
        )
        y = y + bias[0:1, base + chan : base + 2 * chan]
        y = y.reshape(y_high, y_wide, chan) + x[2 : 2 + y_high, 18 - before : 18 - before + y_wide, :]
        skip = before - 2
        ok = inside(y.shape, row * high - skip, row_count * high, me * wide - skip, col_count * wide)
        v[:, 0:y_wide, 0:chan] = rounded(jnp.where(ok, jax.nn.relu(y), 0.0))
        ys.append(v[skip : skip + high, skip : skip + wide, 0:chan].astype(BF16))
    y1_ref[...] = ys[0]
    y2_ref[...] = ys[1]
    s1 = aligned(groups_one(unit))
    off1, off2 = offs[0], offs[1]
    half_high, half_wide = high1 // 2, wide1 // 2
    out_high, out_wide = half_high + 3, up_to(half_wide + 3, 8)
    first = taps(
        (v1,), out_high, out_wide, 2, 0, 0, lambda t: g1[t * unit : (t + 1) * unit, 0 : 4 * unit], (0, unit)
    )
    first = first + bias[0:1, off1 : off1 + 4 * unit]
    s12[...] = first[:, 0 : 2 * unit].reshape(out_high, out_wide, 2 * unit)
    d12_ref[...] = s12[3 : 3 + half_high, 3 : 3 + half_wide, :]
    t = jax.nn.relu(first[:, 2 * unit : 4 * unit]).reshape(out_high, out_wide, 2 * unit)
    ok = inside(
        t.shape, row * half_high - 3, row_count * half_high, me * half_wide - 3, col_count * half_wide
    )
    t1[:, 0:out_wide, 0 : 2 * unit] = rounded(jnp.where(ok, t, 0.0))
    quarter_high, quarter_wide = half_high // 2, half_wide // 2
    d13 = taps(
        (t1,), quarter_high, quarter_wide, 2, 2, 2,
        lambda t: g1[t * unit : (t + 1) * unit, s1[1] : s1[1] + 4 * unit], (0, unit),
    )
    d13 = d13 + bias[0:1, off1 + 4 * unit : off1 + 8 * unit]
    q_high, q_wide = quarter_high + 1, up_to(quarter_wide + 1, 8)
    t14b = taps(
        (t1,), q_high, q_wide, 2, 0, 0,
        lambda t: g1[t * unit : (t + 1) * unit, s1[2] : s1[2] + unit], (unit, 2 * unit),
    )
    t14b = jax.nn.relu(t14b + bias[0:1, off1 + 8 * unit : off1 + 9 * unit]).reshape(q_high, q_wide, unit)
    q_args = (row * quarter_high - 1, row_count * quarter_high, me * quarter_wide - 1, col_count * quarter_wide)
    tb[:, 0:q_wide, 0:unit] = rounded(jnp.where(inside(t14b.shape, *q_args), t14b, 0.0))
    e_high, e_wide = quarter_high // 2, 8
    d14 = taps(
        (tb,), e_high, e_wide, 2, 0, 0,
        lambda t: g1[t * unit : (t + 1) * unit, s1[3] : s1[3] + 8 * unit], (0, unit),
    )
    d14 = d14 + bias[0:1, off1 + 9 * unit : off1 + 17 * unit]
    s2 = aligned(groups_two(unit))
    second = taps(
        (v2,), q_high, q_wide, 2, 0, 0,
        lambda t: g2[t * chan2 : (t + 1) * chan2, 0 : s2[1] + 2 * unit], (0, chan2),
    )
    d23 = second[:, 0 : 4 * unit] + bias[0:1, off2 : off2 + 4 * unit]
    s3[...] = d23.reshape(q_high, q_wide, 4 * unit)
    d3_ref[...] = d13.reshape(quarter_high, quarter_wide, 4 * unit) + s3[
        1 : 1 + quarter_high, 1 : 1 + quarter_wide, :
    ]
    t24 = jax.nn.relu(second[:, s2[1] : s2[1] + 2 * unit] + bias[0:1, off2 + 4 * unit : off2 + 6 * unit])
    t24 = t24.reshape(q_high, q_wide, 2 * unit)
    t2[:, 0:q_wide, 0 : 2 * unit] = rounded(jnp.where(inside(t24.shape, *q_args), t24, 0.0))
    d24 = taps(
        (t2,), e_high, e_wide, 2, 0, 0,
        lambda t: g2[t * chan2 : (t + 1) * chan2, s2[2] : s2[2] + 8 * unit], (0, chan2),
    )
    d24 = d24 + bias[0:1, off2 + 6 * unit : off2 + 14 * unit]
    d4_ref[...] = (d14 + d24).reshape(e_high, e_wide, 8 * unit)


FINE = ("conv_one", "conv_two", "down_one", "down_two")
LAST = ("down_three", "lift_two", "lift_three", "lift_four")


def groups_one(unit):
    return (4 * unit, 4 * unit, unit, 8 * unit)


def groups_two(unit):
    return (4 * unit, 2 * unit, 8 * unit)


def join_kernel(plan, index, *refs):
    packing, count, unit, offs, widths, shapes = plan
    blocks = refs[:count]
    y1_ref, y2_ref, d12_ref, d3_ref, d4_ref, bias = refs[count : count + 6]
    buffers = refs[count + 6 : 2 * count + 6]
    out1, out2, out3, out4 = refs[2 * count + 6 : 2 * count + 10]
    (v3a, v3b, a2, a3a, a3b, a1, p2, p1, c3, k3, l2, l3, l4, stacked, semaphores) = refs[2 * count + 10 :]
    me = index[1]
    copies = fetch(packing, LAST, me, buffers, stacked, semaphores)
    (high2, wide2, chan2), (high3, wide3, chan3), (high4, wide4, chan4) = shapes[1:]
    own3, own4 = chan3 // count, chan4 // count
    cut = (high3 + 1) * 8
    parts = [
        jnp.concatenate([b[0:cut, 0:own3].astype(F32), b[0:cut, 64 : 64 + own3].astype(F32)], axis=0)
        for b in blocks
    ]
    whole3 = natural(parts, me, own3, chan3).reshape(high3 + 1, 16, chan3)
    v3 = (v3a, v3b)
    wide_store(v3, slice(None), slice(0, 16), whole3)
    y4 = natural([b[cut : cut + high4 * 8, 0:own4] for b in blocks], me, own4, chan4)
    y3 = wide_load(v3, slice(1, 1 + high3), slice(1, 1 + wide3))[:, :, 0:chan3]
    for copy in copies:
        copy.wait()
    groups3, groups4 = (unit, 2 * unit), (unit, 2 * unit, 4 * unit)
    packing.assemble("down_three", stacked, widths["down_three"], (chan4,), k3)
    packing.assemble("lift_two", stacked, widths["lift_two"], (unit,), l2)
    packing.assemble("lift_three", stacked, widths["lift_three"], groups3, l3)
    packing.assemble("lift_four", stacked, widths["lift_four"], groups4, l4)
    off3, offl2, offl3, offl4 = offs[2:]

    def lifted(flat, kernel, groups, offset):
        values, first = [], 0
        for group, start in zip(groups, aligned(groups)):
            value = dot(flat, kernel[:, start : start + group])
            values.append(value + bias[0:1, offset + first : offset + first + group])
            first += group
        return values

    def double(scratch, value, keep):
        high, wide, channels = value.shape
        for r in range(2):
            for q in range(2):
                wide_store(scratch, pl.ds(r, high, stride=2), pl.ds(q, wide, stride=2), value)
        return wide_load(scratch, slice(0, 2 * high), slice(0, keep))[:, :, 0:channels]

    u4 = [u.reshape(high4, 8, -1) for u in lifted(y4, l4, groups4, offl4)]
    u3 = [u.reshape(high3, wide3, -1) for u in lifted(y3.reshape(high3 * wide3, chan3), l3, groups3, offl3)]
    y2 = y2_ref[...]
    (u2,) = lifted(y2.reshape(high2 * wide2, chan2), l2, (unit,), offl2)
    d34 = taps(v3, high4, 8, 2, 0, 0, lambda t: k3[t * chan3 : (t + 1) * chan3, 0:chan4], (0, chan3))
    d34 = d34 + bias[0:1, off3 : off3 + chan4]
    four = jax.nn.relu(d4_ref[...] + (d34 + y4).reshape(high4, 8, chan4))
    c3[...] = four
    out4[...] = c3[:, 0:wide4, :].astype(BF16)
    three = double((a3a, a3b), u4[2], wide3) + d3_ref[...] + y3
    out3[...] = jax.nn.relu(three).astype(BF16)
    two = double((a2,), u4[1], wide3) + u3[1]
    two = double((p2,), two, wide2) + d12_ref[...] + y2.astype(F32)
    out2[...] = jax.nn.relu(two).astype(BF16)
    fine = double((a1,), u4[0], wide3) + u3[0]
    fine = double((p1,), fine, wide2) + u2.reshape(high2, wide2, unit)
    fine = double((p1,), fine, shapes[0][1]) + y1_ref[...].astype(F32)
    out1[...] = jax.nn.relu(fine).astype(BF16)


def offsets(width):
    start = 30 * width
    return (
        start,
        start + 17 * width,
        start + 31 * width,
        start + 39 * width,
        start + 40 * width,
        start + 43 * width,
    )


def flipped(value, mask, count):
    return lax.ppermute(value, "cols", [(i, i ^ mask) for i in range(count)])


def shifted(value, axis, distance):
    count = lax.axis_size(axis)
    route = [(i, i + distance) for i in range(count) if 0 <= i + distance < count]
    return lax.ppermute(value, axis, route)


def exchanged(value, count):
    return [value] + [flipped(value, mask, count) for mask in range(1, count)]


def gathered(value, count):
    held = {0: value}
    bits = [1 << b for b in range(1, count.bit_length() - 1)] + ([1] if count > 1 else [])
    for bit in bits:
        for mask in list(held):
            held[mask | bit] = flipped(held[mask], bit, count)
    return [held[mask] for mask in range(count)]


def on_device(
    feat_one,
    feat_two,
    feat_three,
    feat_four,
    conv_one,
    conv_two,
    conv_three,
    conv_four,
    down_one,
    down_two,
    down_three,
    lift_two,
    lift_three,
    lift_four,
    biases,
):
    count = lax.axis_size("cols")
    row_total = lax.axis_size("rows")
    feats = (feat_one, feat_two, feat_three, feat_four)
    shapes = tuple(f.shape for f in feats)
    unit = feat_one.shape[2]
    offs = offsets(unit)
    bias = biases.reshape(1, -1)
    index = jnp.stack(
        [
            lax.axis_index("rows").astype(jnp.int32),
            lax.axis_index("cols").astype(jnp.int32),
            jnp.int32(row_total),
            jnp.int32(count),
        ]
    )
    smem = [pl.BlockSpec(memory_space=pltpu.SMEM)]
    anywhere = [pl.BlockSpec(memory_space=pl.ANY)]
    layouts = (RowLayout(shapes, BEFORE), RowLayout(shapes, (AFTER,) * 4))
    most = max(layouts[0].total, layouts[1].total)
    down, up = pl.pallas_call(
        functools.partial(rows_kernel, layouts),
        out_shape=[jax.ShapeDtypeStruct((l.total, LANES), BF16) for l in layouts],
        in_specs=vmem(4),
        out_specs=vmem(2),
        scratch_shapes=[pltpu.VMEM((most, LANES), F32)],
        compiler_params=PARAMS,
        name="rows_pack",
    )(*feats)
    top = shifted(down, "rows", 1)
    bottom = shifted(up, "rows", -1)

    weights = {
        "conv_one": conv_one,
        "conv_two": conv_two,
        "down_one": down_one,
        "down_two": down_two,
        "down_three": down_three,
        "lift_two": lift_two,
        "lift_three": lift_three,
        "lift_four": lift_four,
    }
    widths = {name: w.shape[1] for name, w in weights.items()}
    packing = Packing({name: w.shape for name, w in weights.items()})
    packed = pl.pallas_call(
        functools.partial(pack_kernel, packing, tuple(weights)),
        out_shape=jax.ShapeDtypeStruct((packing.total, LANES), BF16),
        in_specs=vmem(len(weights)),
        out_specs=pl.BlockSpec(memory_space=pltpu.VMEM),
        compiler_params=PARAMS,
        name="weights_pack",
    )(*weights.values())
    buffers = gathered(packed, count)

    (high1, wide1, chan1), (high2, wide2, chan2), (high3, wide3, chan3), (high4, wide4, chan4) = shapes
    size4 = gather_four(shapes[3])
    total3, head3 = gather_three(shapes[2])
    lanes = max(chan4, 2 * chan3)
    rows1 = high1 + BEFORE[0] + AFTER
    rows2 = high2 + BEFORE[1] + AFTER
    gather, to_right, to_left = pl.pallas_call(
        functools.partial(columns_kernel, layouts),
        out_shape=[
            jax.ShapeDtypeStruct((size4 + head3, lanes), BF16),
            jax.ShapeDtypeStruct((rows1, 16, LANES), BF16),
            jax.ShapeDtypeStruct((rows1, 8, LANES), BF16),
        ],
        in_specs=vmem(6),
        out_specs=vmem(3),
        scratch_shapes=[
            pltpu.VMEM((rows1, wide1, chan1), F32),
            pltpu.VMEM((rows2, wide2, chan2), F32),
            pltpu.VMEM((total3, chan3), F32),
            pltpu.VMEM((size4 + head3, lanes), F32),
            pltpu.VMEM((rows1, 16, LANES), F32),
        ],
        compiler_params=PARAMS,
        name="columns_pack",
    )(*feats, top, bottom)
    coarse = exchanged(gather, count)
    from_left = shifted(to_right, "cols", 1)
    from_right = shifted(to_left, "cols", -1)

    sizes = (count, high3, wide3, chan3, high4, wide4, chan4, 6 * unit, 14 * unit)
    own3, own4 = chan3 // count, chan4 // count
    half, last = message_rows(sizes)
    full_wide3, full_wide4 = up_to(wide3 * count + 2, 8), up_to(wide4 * count + 2, 8)
    mid, res3, res4 = pl.pallas_call(
        functools.partial(coarse_first_kernel, sizes),
        out_shape=[
            jax.ShapeDtypeStruct((last, LANES), BF16),
            jax.ShapeDtypeStruct(((high3 + 1) * wide3 * count, own3), BF16),
            jax.ShapeDtypeStruct((high4 * wide4 * count, own4), BF16),
        ],
        in_specs=smem + vmem(count + 3),
        out_specs=vmem(3),
        scratch_shapes=[
            pltpu.VMEM((high3 + BEFORE[2] + AFTER, full_wide3, chan3), F32),
            pltpu.VMEM((high4 + BEFORE[3] + AFTER, full_wide4, chan4), F32),
            pltpu.VMEM((last, LANES), F32),
        ],
        compiler_params=PARAMS,
        name="coarse_first",
    )(index, *coarse, conv_three, conv_four, bias)
    mids = exchanged(mid, count)
    message = (high3 + 1) * 8 + high4 * 8
    sent = pl.pallas_call(
        functools.partial(coarse_second_kernel, sizes),
        out_shape=[jax.ShapeDtypeStruct((message, LANES), BF16)] * count,
        in_specs=smem + vmem(count + 5),
        out_specs=vmem(count),
        scratch_shapes=[
            pltpu.VMEM((high3 + BEFORE[2] + AFTER - 2, full_wide3, chan3), F32),
            pltpu.VMEM((high4 + BEFORE[3] + AFTER - 2, full_wide4, chan4), F32),
            pltpu.VMEM((message, LANES), F32),
        ],
        compiler_params=PARAMS,
        name="coarse_second",
    )(index, *mids, res3, res4, conv_three, conv_four, bias)
    coarse_out = [sent[0]] + [flipped(sent[mask], mask, count) for mask in range(1, count)]

    plan = (packing, layouts, count, unit, offs, widths)
    mid_wide1, mid_wide2 = up_to(wide1 + BEFORE[0], 8), up_to(wide2 + BEFORE[1], 8)
    y_wide1, y_wide2 = up_to(wide1 + BEFORE[0] - 2, 8), up_to(wide2 + BEFORE[1] - 2, 8)
    half_wide = up_to(wide1 // 2 + 3, 8)
    quarter_wide = up_to(wide1 // 4 + 1, 8)
    fine = pl.pallas_call(
        functools.partial(fine_kernel, plan),
        out_shape=[
            jax.ShapeDtypeStruct(shapes[0], BF16),
            jax.ShapeDtypeStruct(shapes[1], BF16),
            jax.ShapeDtypeStruct((high1 // 2, wide1 // 2, 2 * unit), F32),
            jax.ShapeDtypeStruct((high1 // 4, wide1 // 4, 4 * unit), F32),
            jax.ShapeDtypeStruct((high1 // 8, 8, 8 * unit), F32),
        ],
        in_specs=smem + vmem(7) + anywhere * count,
        out_specs=vmem(5),
        scratch_shapes=[
            pltpu.VMEM((rows1, 24 + mid_wide1, chan1), F32),
            pltpu.VMEM((high1 + BEFORE[0], mid_wide1 + 8, chan1), F32),
            pltpu.VMEM((high1 + BEFORE[0] - 2, 2 * half_wide + 8, LANES), F32),
            pltpu.VMEM((high1 // 2 + 3, max(2 * quarter_wide, half_wide) + 8, LANES), F32),
            pltpu.VMEM((high1 // 4 + 1, max(16, quarter_wide) + 8, LANES), F32),
            pltpu.VMEM((high1 // 2 + 3, half_wide, 2 * unit), F32),
            pltpu.VMEM((rows2, 24 + mid_wide2, chan2), F32),
            pltpu.VMEM((high2 + BEFORE[1], mid_wide2 + 8, chan2), F32),
            pltpu.VMEM((high2 + BEFORE[1] - 2, max(2 * quarter_wide, y_wide2) + 8, LANES), F32),
            pltpu.VMEM((high1 // 4 + 1, max(16, quarter_wide) + 8, LANES), F32),
            pltpu.VMEM((high1 // 4 + 1, quarter_wide, 4 * unit), F32),
            pltpu.VMEM((conv_one.shape[0], LANES), BF16),
            pltpu.VMEM((conv_two.shape[0], LANES), BF16),
            pltpu.VMEM((down_one.shape[0], aligned_width(groups_one(unit))), BF16),
            pltpu.VMEM((down_two.shape[0], aligned_width(groups_two(unit))), BF16),
            pltpu.VMEM((count, packing.total, LANES), BF16),
            pltpu.SemaphoreType.DMA((count, len(packing.ranges(FINE)))),
        ],
        compiler_params=PARAMS,
        name="fine",
    )(index, feat_one, feat_two, top, bottom, from_left, from_right, bias, *buffers)

    plan = (packing, count, unit, offs, widths, shapes)
    return tuple(
        pl.pallas_call(
            functools.partial(join_kernel, plan),
            out_shape=[jax.ShapeDtypeStruct(shape, BF16) for shape in shapes],
            in_specs=smem + vmem(count + 6) + anywhere * count,
            out_specs=vmem(4),
            scratch_shapes=[
                pltpu.VMEM((high3 + 1, 24, LANES), F32),
                pltpu.VMEM((high3 + 1, 24, LANES), F32),
                pltpu.VMEM((2 * high4, 16, LANES), F32),
                pltpu.VMEM((2 * high4, 16, LANES), F32),
                pltpu.VMEM((2 * high4, 16, LANES), F32),
                pltpu.VMEM((2 * high4, 16, LANES), F32),
                pltpu.VMEM((high2, wide2, LANES), F32),
                pltpu.VMEM((high1, wide1, LANES), F32),
                pltpu.VMEM((high4, 8, chan4), F32),
                pltpu.VMEM((down_three.shape[0], up_to(chan4, LANES)), BF16),
                pltpu.VMEM((chan2, LANES), BF16),
                pltpu.VMEM((chan3, aligned_width((unit, 2 * unit))), BF16),
                pltpu.VMEM((chan4, aligned_width((unit, 2 * unit, 4 * unit))), BF16),
                pltpu.VMEM((count, packing.total, LANES), BF16),
                pltpu.SemaphoreType.DMA((count, len(packing.ranges(LAST)))),
            ],
            compiler_params=PARAMS,
            name="join",
        )(index, *coarse_out, *fine, bias, *buffers)
    )


def solution(mesh):
    spatial = P(("win", "rows"), "cols", None)
    placed = (spatial,) * 4 + (P(None, "cols"),) * 10 + (P(),)
    return jax.shard_map(
        on_device,
        mesh=mesh,
        in_specs=placed,
        out_specs=(spatial,) * 4,
        check_vma=False,
    )
```

```python
import functools

import jax
import jax.numpy as jnp
from jax import lax
from jax.experimental import pallas as pl
from jax.experimental.pallas import tpu as pltpu
from jax.sharding import PartitionSpec as P


F32 = jnp.float32
BF16 = jnp.bfloat16
LANES = 128
BEFORE = (9, 5, 3, 2)
AFTER = 2


def up_to(value, multiple):
    return -(-value // multiple) * multiple


def dot(a, b):
    return jnp.dot(a.astype(BF16), b.astype(BF16), preferred_element_type=F32)


def iota(shape, dim):
    return lax.broadcasted_iota(jnp.int32, shape, dim)


def onehot(condition):
    return jnp.where(condition, 1.0, 0.0).astype(F32).astype(BF16)


def dot_t(a, b):
    return lax.dot_general(
        a.astype(BF16), b.astype(BF16), (((1,), (1,)), ((), ())), preferred_element_type=F32
    )


def conv(ref, height, breadth, row, col, weight_of):
    moved = []
    for q in range(3):
        block = ref[row : row + height + 2, col + q : col + q + breadth, :]
        moved.append(block.reshape((height + 2) * breadth, block.shape[2]).astype(BF16))
    wide = jnp.concatenate(moved, axis=1)
    size = height * breadth
    total = None
    for r in range(3):
        part = dot_t(wide[r * breadth : r * breadth + size], weight_of(r))
        total = part if total is None else total + part
    return total


def conv_strided(refs, height, breadth, row, col, lanes, weight_of):
    total = None
    for r in range(3):
        moved = []
        for q in range(3):
            block = wide_load(
                refs, pl.ds(row + r, height, stride=2), pl.ds(col + q, breadth, stride=2)
            )[:, :, lanes[0] : lanes[1]]
            moved.append(block.reshape(height * breadth, block.shape[2]).astype(BF16))
        part = dot_t(jnp.concatenate(moved, axis=1), weight_of(r))
        total = part if total is None else total + part
    return total


def third(kernel, first, last, start, channels):
    step = 3 * channels
    return lambda r: kernel[first:last, start + r * step : start + (r + 1) * step].astype(BF16)


def position():
    return lax.axis_index("rows"), lax.axis_index("cols")


def bias_row(bias_ref, line):
    for r in range(bias_ref.shape[0]):
        line[0:1, r * LANES : (r + 1) * LANES] = bias_ref[r : r + 1, :]


def wide_load(refs, rows, cols):
    parts = [ref[rows, cols, :] for ref in refs]
    return parts[0] if len(parts) == 1 else jnp.concatenate(parts, axis=2)


def wide_store(refs, rows, cols, value):
    channels = value.shape[2]
    for i, ref in enumerate(refs):
        part = value[:, :, i * LANES : min((i + 1) * LANES, channels)]
        if part.shape[2] < LANES:
            rest = jnp.zeros(part.shape[:2] + (LANES - part.shape[2],), part.dtype)
            part = jnp.concatenate([part, rest], axis=2)
        ref[rows, cols, :] = part


def inside(shape, row_first, row_count, col_first, col_count):
    rows = iota(shape, 0) + row_first
    cols = iota(shape, 1) + col_first
    return (rows >= 0) & (rows < row_count) & (cols >= 0) & (cols < col_count)


def rounded(value):
    return value.astype(BF16).astype(F32)


def vmem(count):
    return [pl.BlockSpec(memory_space=pltpu.VMEM)] * count


PARAMS = pltpu.CompilerParams(vmem_limit_bytes=56 * 1024 * 1024)


class RowLayout:
    def __init__(self, shapes, counts):
        self.counts = counts
        self.half = shapes[0][1] // 2
        self.start = []
        at = 0
        for level, ((_, breadth, channels), count) in enumerate(zip(shapes, counts)):
            self.start.append(at)
            positions = count * (self.half if level == 0 else breadth)
            at += positions * (1 if level == 0 else -(-channels // LANES))
        self.total = up_to(at, 16)


def pack_rows(layout, refs, firsts, scratch):
    one, two, three, four = refs
    count = layout.counts
    half = layout.half
    for part in range(2):
        block = one[firsts[0] : firsts[0] + count[0], part * half : (part + 1) * half, :]
        size = count[0] * half
        scratch[0:size, part * 64 : part * 64 + one.shape[2]] = block.astype(F32).reshape(size, -1)
    at = layout.start[1]
    size = count[1] * two.shape[1]
    block = two[firsts[1] : firsts[1] + count[1], :, :].astype(F32).reshape(size, two.shape[2])
    scratch[at : at + size, 0 : two.shape[2]] = block
    at = layout.start[2]
    size = count[2] * three.shape[1]
    block = three[firsts[2] : firsts[2] + count[2], :, :].astype(F32).reshape(size, three.shape[2])
    for low in range(0, three.shape[2], LANES):
        high = min(low + LANES, three.shape[2])
        scratch[at : at + size, 0 : high - low] = block[:, low:high]
        at += size
    breadth = four.shape[1]
    size = count[3] * breadth
    for row in range(count[3]):
        block = four[firsts[3] + row].astype(F32)
        at = layout.start[3] + row * breadth
        for low in range(0, four.shape[2], LANES):
            scratch[at : at + breadth, 0:LANES] = block[:, low : low + LANES]
            at += size


def rows_kernel(layouts, one, two, three, four, down_ref, up_ref, scratch):
    refs = (one, two, three, four)
    low, high = layouts
    firsts = tuple(ref.shape[0] - count for ref, count in zip(refs, low.counts))
    scratch[...] = jnp.zeros_like(scratch)
    pack_rows(low, refs, firsts, scratch)
    down_ref[...] = scratch[0 : low.total, :].astype(BF16)
    pack_rows(high, refs, (0, 0, 0, 0), scratch)
    up_ref[...] = scratch[0 : high.total, :].astype(BF16)


def stretch_fine(level, layout_pair, feat, top, bottom, target, col):
    low, high = layout_pair
    height, breadth, channels = feat.shape
    before, after = low.counts[level], high.counts[level]
    for layout, message, row, count in (
        (low, top, 0, before),
        (high, bottom, before + height, after),
    ):
        at = layout.start[level]
        if level == 0:
            half = layout.half
            for part in range(2):
                block = message[at : at + count * half, part * 64 : part * 64 + channels]
                target[row : row + count, col + part * half : col + (part + 1) * half, :] = (
                    block.astype(F32).reshape(count, half, channels)
                )
        else:
            block = message[at : at + count * breadth, 0:channels]
            target[row : row + count, col : col + breadth, :] = block.astype(F32).reshape(
                count, breadth, channels
            )
    target[before : before + height, col : col + breadth, :] = feat[...].astype(F32)


def columns_kernel(layouts, three, four, top, bottom, after, gather_ref, full_three, message):
    low, high = layouts
    breadth, channels = three.shape[1], three.shape[2]
    own = three.shape[0] * breadth
    before, after = low.counts[2] * breadth, high.counts[2] * breadth
    for layout, source, row, size in ((low, top, 0, before), (high, bottom, before + own, after)):
        at = layout.start[2]
        for first in range(0, channels, LANES):
            last = min(first + LANES, channels)
            full_three[row : row + size, first:last] = source[at : at + size, 0 : last - first].astype(F32)
            at += size
    full_three[before : before + own, :] = three[...].astype(F32).reshape(own, channels)
    size_four = gather_four(four.shape)
    breadth, channels4 = four.shape[1], four.shape[2]
    before, after = low.counts[3] * breadth, high.counts[3] * breadth
    for layout, source, row, size in (
        (low, top, 0, before),
        (high, bottom, before + four.shape[0] * breadth, after),
    ):
        at = layout.start[3]
        for first in range(0, channels4, LANES):
            message[row : row + size, first : first + LANES] = source[at : at + size, :].astype(F32)
            at += size
    for row in range(four.shape[0]):
        at = before + row * breadth
        message[at : at + breadth, 0:channels4] = four[row].astype(F32)
    total, head = gather_three(three.shape)
    message[size_four : size_four + head, 0:channels] = full_three[0:head, :]
    message[size_four : size_four + total - head, channels : 2 * channels] = full_three[head:total, :]
    gather_ref[...] = message[...].astype(BF16)


def edges_kernel(layouts, one, two, top, bottom, after, right_ref, left_ref, full_one, full_two, edge):
    stretch_fine(0, layouts, one, top, bottom, full_one, 0)
    stretch_fine(1, layouts, two, top, bottom, full_two, 0)
    wide, wide_two = one.shape[1], two.shape[1]
    left, left_two = BEFORE[0], BEFORE[1]
    rows_two = full_two.shape[0]
    edge[:, 0:left, 0 : one.shape[2]] = full_one[:, wide - left : wide, :]
    edge[0:rows_two, left : left + left_two, 0 : two.shape[2]] = full_two[
        :, wide_two - left_two : wide_two, :
    ]
    right_ref[...] = edge[...].astype(BF16)
    edge[:, 0:AFTER, 0 : one.shape[2]] = full_one[:, 0:AFTER, :]
    edge[0:rows_two, AFTER : 2 * AFTER, 0 : two.shape[2]] = full_two[:, 0:AFTER, :]
    left_ref[...] = edge[:, 0:8, :].astype(BF16)


def gather_four(shape):
    return (shape[0] + BEFORE[3] + AFTER) * shape[1]


def gather_three(shape):
    total = (shape[0] + BEFORE[2] + AFTER) * shape[1]
    return total, up_to(-(-total // 2), 8)


def own_channels(me, channels, own):
    return onehot(iota((channels, own), 0) == iota((channels, own), 1) + me * own)


def own_bias(line, first, me, own, count):
    total = None
    for j in range(count):
        part = jnp.where(me == j, line[0:1, first + j * own : first + (j + 1) * own], 0.0)
        total = part if total is None else total + part
    return total


def spread(target, blocks, me, rows, block_cols):
    shift = block_cols.bit_length() - 1
    width = target.shape[1]
    total = None
    for k, block in enumerate(blocks):
        size = block.shape[0]
        shape = (rows, width, size)
        source = iota(shape, 2)
        slot = (me ^ k) * block_cols + 1 + (source & (block_cols - 1))
        choose = ((source >> shift) == iota(shape, 0)) & (iota(shape, 1) == slot)
        part = dot(onehot(choose).reshape(rows * width, size), block)
        total = part if total is None else total + part
    target[...] = total.reshape(rows, width, total.shape[1])


def coarse_first_kernel(sizes, *refs):
    count, rows_all, high3, wide3, chan3, high4, wide4, chan4, bias3, bias4 = sizes
    blocks = refs[:count]
    conv3, conv4, bias_ref, _, out, res3, res4, full3, full4, message, line = refs[count:]
    row, me = position()
    bias_row(bias_ref, line)
    size4 = gather_four((high4, wide4))
    total3, head = gather_three((high3, wide3))
    spread(full4, [b[0:size4, 0:chan4] for b in blocks], me, high4 + BEFORE[3] + AFTER, wide4)
    parts = []
    for b in blocks:
        parts.append(
            jnp.concatenate(
                [
                    b[size4 : size4 + head, 0:chan3].astype(F32),
                    b[size4 : size4 + total3 - head, chan3 : 2 * chan3].astype(F32),
                ],
                axis=0,
            )
        )
    spread(full3, parts, me, high3 + BEFORE[2] + AFTER, wide3)
    heights = []
    for full, kernel, high, wide, chan, before, base in (
        (full3, conv3, high3, wide3, chan3, BEFORE[2], bias3),
        (full4, conv4, high4, wide4, chan4, BEFORE[3], bias4),
    ):
        own = chan // count
        out_high = high + before + AFTER - 2
        out_wide = wide * count
        mid = conv(full, out_high, out_wide, 0, 0, third(kernel, 0, own, 0, chan))
        mid = jax.nn.relu(mid + own_bias(line, base, me, own, count)).reshape(out_high, out_wide, own)
        rows = iota(mid.shape, 0) + row * high - (before - 1)
        valid = (rows >= 0) & (rows < rows_all * high)
        heights.append(jnp.where(valid, mid, 0.0).reshape(out_high * out_wide, own))
    mid3, mid4 = heights
    half = mid3.shape[0] // 2
    own3, own4 = mid3.shape[1], mid4.shape[1]
    message[0:half, 0:own3] = mid3[0:half]
    message[0:half, 64 : 64 + own3] = mid3[half:]
    message[half : half + mid4.shape[0], 0:own4] = mid4
    out[...] = message[...].astype(BF16)
    skip3 = BEFORE[2] - 1
    keep = full3[skip3 : skip3 + high3 + 1, 1 : 1 + wide3 * count, :].reshape(-1, chan3)
    res3[...] = dot(keep, own_channels(me, chan3, own3)).astype(BF16)
    keep = full4[BEFORE[3] : BEFORE[3] + high4, 1 : 1 + wide4 * count, :].reshape(-1, chan4)
    res4[...] = dot(keep, own_channels(me, chan4, own4)).astype(BF16)


def natural(blocks, me, own, channels):
    total = None
    for k, block in enumerate(blocks):
        place = onehot(iota((own, channels), 1) == iota((own, channels), 0) + (me ^ k) * own)
        part = dot(block, place)
        total = part if total is None else total + part
    return total


def message_rows(sizes):
    count, _, high3, wide3, _, high4, wide4, _, _, _ = sizes
    half = (high3 + BEFORE[2] + AFTER - 2) * wide3 * count // 2
    return half, half + (high4 + BEFORE[3] + AFTER - 2) * wide4 * count


def coarse_second_kernel(sizes, *refs):
    count, rows_all, high3, wide3, chan3, high4, wide4, chan4, bias3, bias4 = sizes
    blocks = refs[:count]
    res3, res4, conv3, conv4, bias_ref, _ = refs[count : count + 6]
    outs = refs[count + 6 : 2 * count + 6]
    full3, full4, message, line = refs[2 * count + 6 :]
    row, me = position()
    bias_row(bias_ref, line)
    own3, own4 = chan3 // count, chan4 // count
    half, last = message_rows(sizes)
    mids3 = [
        jnp.concatenate([b[0:half, 0:own3].astype(F32), b[0:half, 64 : 64 + own3].astype(F32)], axis=0)
        for b in blocks
    ]
    mids4 = [b[half:last, 0:own4] for b in blocks]
    results = []
    for full, mids, kernel, res, high, wide, chan, before, base, extra in (
        (full3, mids3, conv3, res3, high3, wide3, chan3, BEFORE[2], bias3, 1),
        (full4, mids4, conv4, res4, high4, wide4, chan4, BEFORE[3], bias4, 0),
    ):
        own = chan // count
        mid_high = high + before + AFTER - 2
        out_wide = wide * count
        full[...] = jnp.zeros_like(full)
        full[:, 1 : 1 + out_wide, :] = natural(mids, me, own, chan).reshape(mid_high, out_wide, chan)
        out_high = high + extra
        first = 9 * chan
        y = conv(full, out_high, out_wide, 0, 0, third(kernel, 0, own, first, chan))
        y = y + own_bias(line, base + chan, me, own, count) + res[...].astype(F32)
        y = jax.nn.relu(y).reshape(out_high, out_wide, own)
        rows = iota(y.shape, 0) + row * high - extra
        y = jnp.where((rows >= 0) & (rows < rows_all * high), y, 0.0)
        results.append(y.reshape(out_high * out_wide, own))
    y3, y4 = results
    for k, out in enumerate(outs):
        target = me ^ k
        wide = wide3 * count
        shape = (high3 + 1, 16, y3.shape[0])
        source = iota(shape, 2)
        slot = iota(shape, 1)
        choose = (
            ((source >> (wide.bit_length() - 1)) == iota(shape, 0))
            & ((source & (wide - 1)) == target * wide3 - 1 + slot)
            & (slot < wide3 + 1)
        )
        part = dot(onehot(choose).reshape((high3 + 1) * 16, -1), y3)
        cut = part.shape[0] // 2
        message[0:cut, 0:own3] = part[0:cut]
        message[0:cut, 64 : 64 + own3] = part[cut:]
        wide = wide4 * count
        shape = (high4, 8, y4.shape[0])
        source = iota(shape, 2)
        slot = iota(shape, 1)
        choose = (
            ((source >> (wide.bit_length() - 1)) == iota(shape, 0))
            & ((source & (wide - 1)) == target * wide4 + slot)
            & (slot < wide4)
        )
        part = dot(onehot(choose).reshape(high4 * 8, -1), y4)
        message[cut : cut + high4 * 8, 0:own4] = part
        out[...] = message[...].astype(BF16)


class Packing:
    def __init__(self, shapes):
        self.place = {}
        at = 0
        for name, (rows, width) in shapes.items():
            pad = up_to(width, 16)
            self.place[name] = (at, pad, width, rows)
            at += pad * -(-rows // LANES)
        self.total = at

    def tiles(self, name):
        at, pad, width, rows = self.place[name]
        for low in range(0, rows, LANES):
            yield at + low // LANES * pad, width, low, min(LANES, rows - low)

    def span(self, names):
        ends = [(self.place[n][0], self.place[n][0] + self.place[n][1] * -(-self.place[n][3] // LANES)) for n in names]
        return min(e[0] for e in ends), max(e[1] for e in ends)

    def scratch(self, name, count):
        _, _, width, rows = self.place[name]
        return pltpu.VMEM((width * count, rows), BF16 if width % 16 == 0 else F32)

    def unpack(self, name, stacked, base, target):
        for j in range(stacked.shape[0]):
            for at, width, low, size in self.tiles(name):
                target[j * width : (j + 1) * width, low : low + size] = stacked[
                    j, at - base : at - base + width, 0:size
                ].astype(target.dtype)


def pack_kernel(packings, *refs):
    inputs = sum(len(p.place) for p in packings)
    sources, outs = iter(refs[:inputs]), refs[inputs + 1 :]
    for packing, out in zip(packings, outs):
        for name in packing.place:
            source = next(sources)
            for at, width, low, size in packing.tiles(name):
                out[at : at + width, 0:size] = source[:, low : low + size]


def fetch(span, me, buffers, stacked, semaphores):
    copies = []
    for k, buffer in enumerate(buffers):
        copy = pltpu.make_async_copy(
            buffer.at[pl.ds(span[0], span[1] - span[0])], stacked.at[me ^ k], semaphores.at[k]
        )
        copy.start()
        copies.append(copy)
    return copies


def fine_kernel(plan, *refs):
    packing, layouts, count, rows_all, unit = plan
    one, two, top, bottom, from_left, from_right, bias_ref, _ = refs[:8]
    buffers = refs[8 : 8 + count]
    y1_ref, y2_ref, v1, v2 = refs[8 + count : 12 + count]
    x1, m1, x2, m2, k1, k2, stacked, line, semaphores = refs[12 + count :]
    row, me = position()
    copies = fetch((0, packing.total), me, buffers, stacked, semaphores)
    bias_row(bias_ref, line)
    high1, wide1, chan1 = one.shape
    high2, wide2, chan2 = two.shape
    stretch_fine(0, layouts, one, top, bottom, x1, 16)
    stretch_fine(1, layouts, two, top, bottom, x2, 16)
    b1, b2 = BEFORE[0], BEFORE[1]
    rows2 = high2 + b2 + AFTER
    x1[:, 16 - b1 : 16, :] = from_left[:, 0:b1, 0:chan1].astype(F32)
    x1[:, 16 + wide1 : 16 + wide1 + AFTER, :] = from_right[:, 0:AFTER, 0:chan1].astype(F32)
    x2[:, 16 - b2 : 16, :] = from_left[0:rows2, b1 : b1 + b2, 0:chan2].astype(F32)
    x2[:, 16 + wide2 : 16 + wide2 + AFTER, :] = from_right[
        0:rows2, AFTER : 2 * AFTER, 0:chan2
    ].astype(F32)
    for copy in copies:
        copy.wait()
    packing.unpack("conv_one", stacked, 0, k1)
    packing.unpack("conv_two", stacked, 0, k2)
    ys = []
    for x, m, v, k, before, high, wide, chan, base in (
        (x1, m1, v1, k1, b1, high1, wide1, chan1, 0),
        (x2, m2, v2, k2, b2, high2, wide2, chan2, 2 * unit),
    ):
        mid_high = high + before
        mid_wide = up_to(wide + before, 16)
        mid = conv(x, mid_high, mid_wide, 0, 16 - before, third(k, 0, chan, 0, chan))
        mid = jax.nn.relu(mid + line[0:1, base : base + chan]).reshape(mid_high, mid_wide, chan)
        ok = inside(
            mid.shape, row * high - before + 1, rows_all * high, me * wide - before + 1, count * wide
        )
        m[:, 0:mid_wide, :] = rounded(jnp.where(ok, mid, 0.0))
        y_high = high + before - 2
        y_wide = up_to(wide + before - 2, 16)
        y = conv(m, y_high, y_wide, 0, 0, third(k, 0, chan, 9 * chan, chan))
        y = y + line[0:1, base + chan : base + 2 * chan]
        y = y.reshape(y_high, y_wide, chan) + x[2 : 2 + y_high, 18 - before : 18 - before + y_wide, :]
        skip = before - 2
        ok = inside(y.shape, row * high - skip, rows_all * high, me * wide - skip, count * wide)
        v[:, 0:y_wide, 0:chan] = rounded(jnp.where(ok, jax.nn.relu(y), 0.0))
        ys.append(v[skip : skip + high, skip : skip + wide, 0:chan].astype(BF16))
    y1_ref[...] = ys[0]
    y2_ref[...] = ys[1]


def down_kernel(plan, *refs):
    packing, count, rows_all, unit, offs, shapes = plan
    v1, v2, bias_ref, _ = refs[:4]
    buffers = refs[4 : 4 + count]
    d12_ref, d3_ref, d4_ref = refs[4 + count : 7 + count]
    t1, tb, s12, t2, s3, g1, g2, stacked, line, semaphores = refs[7 + count :]
    row, me = position()
    span = packing.span(("down_one", "down_two"))
    copies = fetch(span, me, buffers, stacked, semaphores)
    bias_row(bias_ref, line)
    for copy in copies:
        copy.wait()
    packing.unpack("down_one", stacked, span[0], g1)
    packing.unpack("down_two", stacked, span[0], g2)
    (high1, wide1, _), (_, _, chan2) = shapes[:2]
    off1, off2 = offs[0], offs[1]
    half_high, half_wide = high1 // 2, wide1 // 2
    out_high, out_wide = half_high + 3, up_to(half_wide + 3, 8)
    first = conv_strided((v1,), out_high, out_wide, 0, 0, (0, unit), third(g1, 0, 4 * unit, 0, unit))
    first = first + line[0:1, off1 : off1 + 4 * unit]
    s12[...] = first[:, 0 : 2 * unit].reshape(out_high, out_wide, 2 * unit)
    d12_ref[...] = s12[3 : 3 + half_high, 3 : 3 + half_wide, :]
    t = jax.nn.relu(first[:, 2 * unit : 4 * unit]).reshape(out_high, out_wide, 2 * unit)
    ok = inside(t.shape, row * half_high - 3, rows_all * half_high, me * half_wide - 3, count * half_wide)
    t1[:, 0:out_wide, 0 : 2 * unit] = rounded(jnp.where(ok, t, 0.0))
    quarter_high, quarter_wide = half_high // 2, half_wide // 2
    d13 = conv_strided(
        (t1,), quarter_high, quarter_wide, 2, 2, (0, unit), third(g1, 4 * unit, 8 * unit, 0, unit)
    )
    d13 = d13 + line[0:1, off1 + 4 * unit : off1 + 8 * unit]
    q_high, q_wide = quarter_high + 1, up_to(quarter_wide + 1, 8)
    t14b = conv_strided((t1,), q_high, q_wide, 0, 0, (unit, 2 * unit), third(g1, 8 * unit, 9 * unit, 0, unit))
    t14b = jax.nn.relu(t14b + line[0:1, off1 + 8 * unit : off1 + 9 * unit]).reshape(q_high, q_wide, unit)
    q_args = (row * quarter_high - 1, rows_all * quarter_high, me * quarter_wide - 1, count * quarter_wide)
    tb[:, 0:q_wide, 0:unit] = rounded(jnp.where(inside(t14b.shape, *q_args), t14b, 0.0))
    e_high, e_wide = quarter_high // 2, 8
    d14 = conv_strided((tb,), e_high, e_wide, 0, 0, (0, unit), third(g1, 9 * unit, 17 * unit, 0, unit))
    d14 = d14 + line[0:1, off1 + 9 * unit : off1 + 17 * unit]
    second = conv_strided((v2,), q_high, q_wide, 0, 0, (0, chan2), third(g2, 0, 6 * unit, 0, chan2))
    second = second + line[0:1, off2 : off2 + 6 * unit]
    s3[...] = second[:, 0 : 4 * unit].reshape(q_high, q_wide, 4 * unit)
    d3_ref[...] = d13.reshape(quarter_high, quarter_wide, 4 * unit) + s3[
        1 : 1 + quarter_high, 1 : 1 + quarter_wide, :
    ]
    t24 = jax.nn.relu(second[:, 4 * unit : 6 * unit]).reshape(q_high, q_wide, 2 * unit)
    t2[:, 0:q_wide, 0 : 2 * unit] = rounded(jnp.where(inside(t24.shape, *q_args), t24, 0.0))
    d24 = conv_strided((t2,), e_high, e_wide, 0, 0, (0, 2 * unit), third(g2, 6 * unit, 14 * unit, 0, chan2))
    d24 = d24 + line[0:1, off2 + 6 * unit : off2 + 14 * unit]
    d4_ref[...] = (d14 + d24).reshape(e_high, e_wide, 8 * unit)


LAST = ("down_three", "lift_two", "lift_three", "lift_four")


def join_kernel(plan, *refs):
    packing, count, unit, offs, shapes = plan
    blocks = refs[:count]
    y1_ref, y2_ref, d12_ref, d3_ref, d4_ref, bias_ref = refs[count : count + 6]
    buffers = refs[count + 6 : 2 * count + 6]
    out1, out2, out3, out4 = refs[2 * count + 6 : 2 * count + 10]
    (v3a, v3b, a2, a3a, a3b, a1, p2, p1, c3, k3, l2, l3, l4, stacked, line, semaphores) = refs[2 * count + 10 :]
    _, me = position()
    span = packing.span(LAST)
    copies = fetch(span, me, buffers, stacked, semaphores)
    bias_row(bias_ref, line)
    (high2, wide2, chan2), (high3, wide3, chan3), (high4, wide4, chan4) = shapes[1:]
    own3, own4 = chan3 // count, chan4 // count
    cut = (high3 + 1) * 8
    parts = [
        jnp.concatenate([b[0:cut, 0:own3].astype(F32), b[0:cut, 64 : 64 + own3].astype(F32)], axis=0)
        for b in blocks
    ]
    whole3 = natural(parts, me, own3, chan3).reshape(high3 + 1, 16, chan3)
    v3 = (v3a, v3b)
    wide_store(v3, slice(None), slice(0, 16), whole3)
    y4 = natural([b[cut : cut + high4 * 8, 0:own4] for b in blocks], me, own4, chan4)
    y3 = wide_load(v3, slice(1, 1 + high3), slice(1, 1 + wide3))[:, :, 0:chan3]
    for copy in copies:
        copy.wait()
    groups3, groups4 = (unit, 2 * unit), (unit, 2 * unit, 4 * unit)
    for name, target in zip(LAST, (k3, l2, l3, l4)):
        packing.unpack(name, stacked, span[0], target)
    off3, offl2, offl3, offl4 = offs[2:]

    def lifted(flat, kernel, groups, offset):
        values, first = [], 0
        for group in groups:
            value = dot_t(flat, kernel[first : first + group, :])
            values.append(value + line[0:1, offset + first : offset + first + group])
            first += group
        return values

    def double(scratch, value, keep):
        high, wide, channels = value.shape
        for r in range(2):
            for q in range(2):
                wide_store(scratch, pl.ds(r, high, stride=2), pl.ds(q, wide, stride=2), value)
        return wide_load(scratch, slice(0, 2 * high), slice(0, keep))[:, :, 0:channels]

    u4 = [u.reshape(high4, 8, -1) for u in lifted(y4, l4, groups4, offl4)]
    u3 = [u.reshape(high3, wide3, -1) for u in lifted(y3.reshape(high3 * wide3, chan3), l3, groups3, offl3)]
    y2 = y2_ref[...]
    (u2,) = lifted(y2.reshape(high2 * wide2, chan2), l2, (unit,), offl2)
    d34 = conv_strided(v3, high4, 8, 0, 0, (0, chan3), third(k3, 0, chan4, 0, chan3))
    d34 = d34 + line[0:1, off3 : off3 + chan4]
    four = jax.nn.relu(d4_ref[...] + (d34 + y4).reshape(high4, 8, chan4))
    c3[...] = four
    out4[...] = c3[:, 0:wide4, :].astype(BF16)
    three = double((a3a, a3b), u4[2], wide3) + d3_ref[...] + y3
    out3[...] = jax.nn.relu(three).astype(BF16)
    two = double((a2,), u4[1], wide3) + u3[1]
    two = double((p2,), two, wide2) + d12_ref[...] + y2.astype(F32)
    out2[...] = jax.nn.relu(two).astype(BF16)
    fine = double((a1,), u4[0], wide3) + u3[0]
    fine = double((p1,), fine, wide2) + u2.reshape(high2, wide2, unit)
    fine = double((p1,), fine, shapes[0][1]) + y1_ref[...].astype(F32)
    out1[...] = jax.nn.relu(fine).astype(BF16)


def offsets(width):
    start = 30 * width
    return (
        start,
        start + 17 * width,
        start + 31 * width,
        start + 39 * width,
        start + 40 * width,
        start + 43 * width,
    )


def flipped(value, mask, count):
    return lax.ppermute(value, "cols", [(i, i ^ mask) for i in range(count)])


def shifted(value, axis, distance):
    count = lax.axis_size(axis)
    route = [(i, i + distance) for i in range(count) if 0 <= i + distance < count]
    return lax.ppermute(value, axis, route)


def exchanged(value, count):
    return [value] + [flipped(value, mask, count) for mask in range(1, count)]


def gathered(value, count):
    held = {0: value}
    for b in range(1, count.bit_length() - 1):
        for mask in list(held):
            held[mask | 1 << b] = flipped(held[mask], 1 << b, count)
    if count > 1:
        for mask in list(held):
            held[mask | 1] = flipped(held[mask], 1, count)
    return [held[mask] for mask in range(count)]


def local(kernel, cost, outs, scratch, operands, anywhere=()):
    return pl.pallas_call(
        kernel,
        out_shape=list(outs),
        in_specs=vmem(len(operands)) + [pl.BlockSpec(memory_space=pl.ANY)] * len(anywhere),
        out_specs=vmem(len(outs)),
        scratch_shapes=scratch,
        compiler_params=PARAMS,
        cost_estimate=pl.CostEstimate(flops=int(cost * 1.15e9), bytes_accessed=0, transcendentals=0),
    )(*operands, *anywhere)


def on_device(
    feat_one,
    feat_two,
    feat_three,
    feat_four,
    conv_one,
    conv_two,
    conv_three,
    conv_four,
    down_one,
    down_two,
    down_three,
    lift_two,
    lift_three,
    lift_four,
    biases,
):
    count = lax.axis_size("cols")
    row_total = lax.axis_size("rows")
    feats = (feat_one, feat_two, feat_three, feat_four)
    shapes = tuple(f.shape for f in feats)
    unit = feat_one.shape[2]
    offs = offsets(unit)
    lines = biases.shape[0] // LANES
    bias = biases.reshape(lines, LANES)
    line = pltpu.VMEM((8, lines * LANES), F32)
    layouts = (RowLayout(shapes, BEFORE), RowLayout(shapes, (AFTER,) * 4))
    most = max(layouts[0].total, layouts[1].total)
    down, up = local(
        functools.partial(rows_kernel, layouts),
        1.5,
        [jax.ShapeDtypeStruct((l.total, LANES), BF16) for l in layouts],
        [pltpu.VMEM((most, LANES), F32)],
        feats,
    )
    top = shifted(down, "rows", 1)
    bottom = shifted(up, "rows", -1)

    early = {"conv_one": conv_one, "conv_two": conv_two}
    late = {
        "down_one": down_one,
        "down_two": down_two,
        "down_three": down_three,
        "lift_two": lift_two,
        "lift_three": lift_three,
        "lift_four": lift_four,
    }
    packings = [Packing({name: w.shape for name, w in group.items()}) for group in (early, late)]
    packed = local(
        functools.partial(pack_kernel, packings),
        1.5,
        [jax.ShapeDtypeStruct((p.total, LANES), BF16) for p in packings],
        [],
        [w.T for group in (early, late) for w in group.values()],
        [down],
    )
    early_buffers = gathered(packed[0], count)

    (high1, wide1, chan1), (high2, wide2, chan2), (high3, wide3, chan3), (high4, wide4, chan4) = shapes
    size4 = gather_four(shapes[3])
    total3, head3 = gather_three(shapes[2])
    lanes = max(chan4, 2 * chan3)
    rows1 = high1 + BEFORE[0] + AFTER
    rows2 = high2 + BEFORE[1] + AFTER
    (gather,) = local(
        functools.partial(columns_kernel, layouts),
        1.0,
        [jax.ShapeDtypeStruct((size4 + head3, lanes), BF16)],
        [pltpu.VMEM((total3, chan3), F32), pltpu.VMEM((size4 + head3, lanes), F32)],
        (feat_three, feat_four, top, bottom),
        [packed[1]],
    )
    coarse = exchanged(gather, count)
    to_right, to_left = local(
        functools.partial(edges_kernel, layouts),
        1.5,
        [jax.ShapeDtypeStruct((rows1, 16, LANES), BF16), jax.ShapeDtypeStruct((rows1, 8, LANES), BF16)],
        [
            pltpu.VMEM((rows1, wide1, chan1), F32),
            pltpu.VMEM((rows2, wide2, chan2), F32),
            pltpu.VMEM((rows1, 16, LANES), F32),
        ],
        (feat_one, feat_two, top, bottom),
        [gather],
    )
    from_left = shifted(to_right, "cols", 1)
    from_right = shifted(to_left, "cols", -1)

    sizes = (count, row_total, high3, wide3, chan3, high4, wide4, chan4, 6 * unit, 14 * unit)
    own3, own4 = chan3 // count, chan4 // count
    _, last = message_rows(sizes)
    full_wide3, full_wide4 = up_to(wide3 * count + 2, 8), up_to(wide4 * count + 2, 8)
    three_t, four_t = conv_three.T, conv_four.T
    mid, res3, res4 = local(
        functools.partial(coarse_first_kernel, sizes),
        3.0,
        [
            jax.ShapeDtypeStruct((last, LANES), BF16),
            jax.ShapeDtypeStruct(((high3 + 1) * wide3 * count, own3), BF16),
            jax.ShapeDtypeStruct((high4 * wide4 * count, own4), BF16),
        ],
        [
            pltpu.VMEM((high3 + BEFORE[2] + AFTER, full_wide3, chan3), F32),
            pltpu.VMEM((high4 + BEFORE[3] + AFTER, full_wide4, chan4), F32),
            pltpu.VMEM((last, LANES), F32),
            line,
        ],
        (*coarse, three_t, four_t, bias),
        [to_right],
    )
    mids = exchanged(mid, count)

    mid_wide1, mid_wide2 = up_to(wide1 + BEFORE[0], 16), up_to(wide2 + BEFORE[1], 16)
    y_wide1, y_wide2 = up_to(wide1 + BEFORE[0] - 2, 16), up_to(wide2 + BEFORE[1] - 2, 16)
    half_wide = up_to(wide1 // 2 + 3, 8)
    quarter_wide = up_to(wide1 // 4 + 1, 8)
    y1, y2, v1, v2 = local(
        functools.partial(fine_kernel, (packings[0], layouts, count, row_total, unit)),
        5.0,
        [
            jax.ShapeDtypeStruct(shapes[0], BF16),
            jax.ShapeDtypeStruct(shapes[1], BF16),
            jax.ShapeDtypeStruct((high1 + BEFORE[0] - 2, max(2 * half_wide, y_wide1) + 8, LANES), F32),
            jax.ShapeDtypeStruct((high2 + BEFORE[1] - 2, max(2 * quarter_wide, y_wide2) + 8, LANES), F32),
        ],
        [
            pltpu.VMEM((rows1, 24 + mid_wide1, chan1), F32),
            pltpu.VMEM((high1 + BEFORE[0], max(mid_wide1, y_wide1) + 8, chan1), F32),
            pltpu.VMEM((rows2, 24 + mid_wide2, chan2), F32),
            pltpu.VMEM((high2 + BEFORE[1], max(mid_wide2, y_wide2) + 8, chan2), F32),
            packings[0].scratch("conv_one", count),
            packings[0].scratch("conv_two", count),
            pltpu.VMEM((count, packings[0].total, LANES), BF16),
            line,
            pltpu.SemaphoreType.DMA((count,)),
        ],
        (feat_one, feat_two, top, bottom, from_left, from_right, bias),
        [mid, *early_buffers],
    )

    message = (high3 + 1) * 8 + high4 * 8
    sent = local(
        functools.partial(coarse_second_kernel, sizes),
        3.0,
        [jax.ShapeDtypeStruct((message, LANES), BF16)] * count,
        [
            pltpu.VMEM((high3 + BEFORE[2] + AFTER - 2, full_wide3, chan3), F32),
            pltpu.VMEM((high4 + BEFORE[3] + AFTER - 2, full_wide4, chan4), F32),
            pltpu.VMEM((message, LANES), F32),
            line,
        ],
        (*mids, res3, res4, three_t, four_t, bias),
        [y1],
    )
    coarse_out = [sent[0]] + [flipped(sent[mask], mask, count) for mask in range(1, count)]
    late_buffers = gathered(packed[1], count)

    span = packings[1].span(("down_one", "down_two"))
    downs = local(
        functools.partial(down_kernel, (packings[1], count, row_total, unit, offs, shapes)),
        5.0,
        [
            jax.ShapeDtypeStruct((high1 // 2, wide1 // 2, 2 * unit), F32),
            jax.ShapeDtypeStruct((high1 // 4, wide1 // 4, 4 * unit), F32),
            jax.ShapeDtypeStruct((high1 // 8, 8, 8 * unit), F32),
        ],
        [
            pltpu.VMEM((high1 // 2 + 3, max(2 * quarter_wide, half_wide) + 8, LANES), F32),
            pltpu.VMEM((high1 // 4 + 1, max(16, quarter_wide) + 8, LANES), F32),
            pltpu.VMEM((high1 // 2 + 3, half_wide, 2 * unit), F32),
            pltpu.VMEM((high1 // 4 + 1, max(16, quarter_wide) + 8, LANES), F32),
            pltpu.VMEM((high1 // 4 + 1, quarter_wide, 4 * unit), F32),
            packings[1].scratch("down_one", count),
            packings[1].scratch("down_two", count),
            pltpu.VMEM((count, span[1] - span[0], LANES), BF16),
            line,
            pltpu.SemaphoreType.DMA((count,)),
        ],
        (v1, v2, bias),
        [sent[0], *late_buffers],
    )

    span = packings[1].span(LAST)
    return tuple(
        local(
            functools.partial(join_kernel, (packings[1], count, unit, offs, shapes)),
            4.0,
            [jax.ShapeDtypeStruct(shape, BF16) for shape in shapes],
            [
                pltpu.VMEM((high3 + 1, 24, LANES), F32),
                pltpu.VMEM((high3 + 1, 24, LANES), F32),
                pltpu.VMEM((2 * high4, 16, LANES), F32),
                pltpu.VMEM((2 * high4, 16, LANES), F32),
                pltpu.VMEM((2 * high4, 16, LANES), F32),
                pltpu.VMEM((2 * high4, 16, LANES), F32),
                pltpu.VMEM((high2, wide2, LANES), F32),
                pltpu.VMEM((high1, wide1, LANES), F32),
                pltpu.VMEM((high4, 8, chan4), F32),
                *[packings[1].scratch(name, count) for name in LAST],
                pltpu.VMEM((count, span[1] - span[0], LANES), BF16),
                line,
                pltpu.SemaphoreType.DMA((count,)),
            ],
            (*coarse_out, y1, y2, *downs, bias),
            late_buffers,
        )
    )


def solution(mesh):
    spatial = P(("win", "rows"), "cols", None)
    placed = (spatial,) * 4 + (P(None, "cols"),) * 10 + (P(),)
    return jax.shard_map(
        on_device,
        mesh=mesh,
        in_specs=placed,
        out_specs=(spatial,) * 4,
        check_vma=False,
    )
```

```python
import functools

import jax
import jax.numpy as jnp
from jax import lax
from jax.experimental import pallas as pl
from jax.experimental.pallas import tpu as pltpu
from jax.sharding import PartitionSpec as P


F32 = jnp.float32
BF16 = jnp.bfloat16
LANES = 128
BEFORE = (9, 5, 3, 2)
AFTER = 2


def up_to(value, multiple):
    return -(-value // multiple) * multiple


def dot(a, b):
    return jnp.dot(a.astype(BF16), b.astype(BF16), preferred_element_type=F32)


def iota(shape, dim):
    return lax.broadcasted_iota(jnp.int32, shape, dim)


def onehot(condition):
    return jnp.where(condition, 1.0, 0.0).astype(F32).astype(BF16)


def dot_t(a, b):
    return lax.dot_general(
        a.astype(BF16), b.astype(BF16), (((1,), (1,)), ((), ())), preferred_element_type=F32
    )


def conv(ref, height, breadth, row, col, weight_of):
    moved = []
    for q in range(3):
        block = ref[row : row + height + 2, col + q : col + q + breadth, :]
        moved.append(block.reshape((height + 2) * breadth, block.shape[2]).astype(BF16))
    wide = jnp.concatenate(moved, axis=1)
    size = height * breadth
    total = None
    for r in range(3):
        part = dot_t(wide[r * breadth : r * breadth + size], weight_of(r))
        total = part if total is None else total + part
    return total


def conv_strided(refs, height, breadth, row, col, lanes, weight_of):
    total = None
    for r in range(3):
        moved = []
        for q in range(3):
            block = wide_load(
                refs, pl.ds(row + r, height, stride=2), pl.ds(col + q, breadth, stride=2)
            )[:, :, lanes[0] : lanes[1]]
            moved.append(block.reshape(height * breadth, block.shape[2]).astype(BF16))
        part = dot_t(jnp.concatenate(moved, axis=1), weight_of(r))
        total = part if total is None else total + part
    return total


def third(kernel, first, last, start, channels):
    step = 3 * channels
    return lambda r: kernel[first:last, start + r * step : start + (r + 1) * step].astype(BF16)


def position():
    return lax.axis_index("rows"), lax.axis_index("cols")


def bias_row(bias_ref, line):
    for r in range(bias_ref.shape[0]):
        line[0:1, r * LANES : (r + 1) * LANES] = bias_ref[r : r + 1, :]


def wide_load(refs, rows, cols):
    parts = [ref[rows, cols, :] for ref in refs]
    return parts[0] if len(parts) == 1 else jnp.concatenate(parts, axis=2)


def wide_store(refs, rows, cols, value):
    channels = value.shape[2]
    for i, ref in enumerate(refs):
        part = value[:, :, i * LANES : min((i + 1) * LANES, channels)]
        if part.shape[2] < LANES:
            rest = jnp.zeros(part.shape[:2] + (LANES - part.shape[2],), part.dtype)
            part = jnp.concatenate([part, rest], axis=2)
        ref[rows, cols, :] = part


def inside(shape, row_first, row_count, col_first, col_count):
    rows = iota(shape, 0) + row_first
    cols = iota(shape, 1) + col_first
    return (rows >= 0) & (rows < row_count) & (cols >= 0) & (cols < col_count)


def rounded(value):
    return value.astype(BF16).astype(F32)


def vmem(count):
    return [pl.BlockSpec(memory_space=pltpu.VMEM)] * count


PARAMS = pltpu.CompilerParams(vmem_limit_bytes=56 * 1024 * 1024)


class RowLayout:
    def __init__(self, shapes, counts):
        self.counts = counts
        self.half = shapes[0][1] // 2
        self.start = []
        at = 0
        for level, ((_, breadth, channels), count) in enumerate(zip(shapes, counts)):
            self.start.append(at)
            positions = count * (self.half if level == 0 else breadth)
            at += positions * (1 if level == 0 else -(-channels // LANES))
        self.total = up_to(at, 16)


def pack_rows(layout, refs, firsts, scratch):
    one, two, three, four = refs
    count = layout.counts
    half = layout.half
    for part in range(2):
        block = one[firsts[0] : firsts[0] + count[0], part * half : (part + 1) * half, :]
        size = count[0] * half
        scratch[0:size, part * 64 : part * 64 + one.shape[2]] = block.astype(F32).reshape(size, -1)
    at = layout.start[1]
    size = count[1] * two.shape[1]
    block = two[firsts[1] : firsts[1] + count[1], :, :].astype(F32).reshape(size, two.shape[2])
    scratch[at : at + size, 0 : two.shape[2]] = block
    at = layout.start[2]
    size = count[2] * three.shape[1]
    block = three[firsts[2] : firsts[2] + count[2], :, :].astype(F32).reshape(size, three.shape[2])
    for low in range(0, three.shape[2], LANES):
        high = min(low + LANES, three.shape[2])
        scratch[at : at + size, 0 : high - low] = block[:, low:high]
        at += size
    breadth = four.shape[1]
    size = count[3] * breadth
    for row in range(count[3]):
        block = four[firsts[3] + row].astype(F32)
        at = layout.start[3] + row * breadth
        for low in range(0, four.shape[2], LANES):
            scratch[at : at + breadth, 0:LANES] = block[:, low : low + LANES]
            at += size


def rows_kernel(layouts, one, two, three, four, even_ref, odd_ref, scratch):
    refs = (one, two, three, four)
    low, high = layouts
    firsts = tuple(ref.shape[0] - count for ref, count in zip(refs, low.counts))
    row, _ = position()
    scratch[...] = jnp.zeros_like(scratch)
    pack_rows(low, refs, firsts, scratch)
    last_rows = scratch[...].astype(BF16)
    pack_rows(high, refs, (0, 0, 0, 0), scratch)
    first_rows = scratch[...].astype(BF16)
    even_ref[...] = jnp.where((row & 1) == 0, last_rows, first_rows)
    odd_ref[...] = jnp.where((row & 1) == 0, first_rows, last_rows)


class Border:
    def __init__(self, even, odd, index):
        self.even, self.odd, self.is_odd = even, odd, (index & 1) == 1

    def prev(self, *at):
        return jnp.where(self.is_odd, self.even[at], self.odd[at]).astype(F32)

    def next(self, *at):
        return jnp.where(self.is_odd, self.odd[at], self.even[at]).astype(F32)


def stretch_fine(level, layout_pair, feat, border, target, col):
    low, high = layout_pair
    height, breadth, channels = feat.shape
    before, after = low.counts[level], high.counts[level]
    for layout, message, row, count in (
        (low, border.prev, 0, before),
        (high, border.next, before + height, after),
    ):
        at = layout.start[level]
        if level == 0:
            half = layout.half
            for part in range(2):
                block = message(slice(at, at + count * half), slice(part * 64, part * 64 + channels))
                target[row : row + count, col + part * half : col + (part + 1) * half, :] = (
                    block.reshape(count, half, channels)
                )
        else:
            block = message(slice(at, at + count * breadth), slice(0, channels))
            target[row : row + count, col : col + breadth, :] = block.reshape(count, breadth, channels)
    target[before : before + height, col : col + breadth, :] = feat[...].astype(F32)


def columns_kernel(layouts, three, four, even, odd, after, gather_ref, full_three, message):
    low, high = layouts
    border = Border(even, odd, position()[0])
    breadth, channels = three.shape[1], three.shape[2]
    own = three.shape[0] * breadth
    before, after = low.counts[2] * breadth, high.counts[2] * breadth
    for layout, source, row, size in (
        (low, border.prev, 0, before),
        (high, border.next, before + own, after),
    ):
        at = layout.start[2]
        for first in range(0, channels, LANES):
            last = min(first + LANES, channels)
            full_three[row : row + size, first:last] = source(slice(at, at + size), slice(0, last - first))
            at += size
    full_three[before : before + own, :] = three[...].astype(F32).reshape(own, channels)
    size_four = gather_four(four.shape)
    breadth, channels4 = four.shape[1], four.shape[2]
    before, after = low.counts[3] * breadth, high.counts[3] * breadth
    for layout, source, row, size in (
        (low, border.prev, 0, before),
        (high, border.next, before + four.shape[0] * breadth, after),
    ):
        at = layout.start[3]
        for first in range(0, channels4, LANES):
            message[row : row + size, first : first + LANES] = source(slice(at, at + size), slice(0, LANES))
            at += size
    for row in range(four.shape[0]):
        at = before + row * breadth
        message[at : at + breadth, 0:channels4] = four[row].astype(F32)
    total, head = gather_three(three.shape)
    message[size_four : size_four + head, 0:channels] = full_three[0:head, :]
    message[size_four : size_four + total - head, channels : 2 * channels] = full_three[head:total, :]
    gather_ref[...] = message[...].astype(BF16)


def edges_kernel(layouts, one, two, even, odd, after, even_ref, odd_ref, full_one, full_two, edge):
    row, me = position()
    border = Border(even, odd, row)
    stretch_fine(0, layouts, one, border, full_one, 0)
    stretch_fine(1, layouts, two, border, full_two, 0)
    wide, wide_two = one.shape[1], two.shape[1]
    left, left_two = BEFORE[0], BEFORE[1]
    rows_two = full_two.shape[0]
    edge[...] = jnp.zeros_like(edge)
    edge[:, 0:left, 0 : one.shape[2]] = full_one[:, wide - left : wide, :]
    edge[0:rows_two, left : left + left_two, 0 : two.shape[2]] = full_two[
        :, wide_two - left_two : wide_two, :
    ]
    last_columns = edge[...].astype(BF16)
    edge[:, 0:AFTER, 0 : one.shape[2]] = full_one[:, 0:AFTER, :]
    edge[0:rows_two, AFTER : 2 * AFTER, 0 : two.shape[2]] = full_two[:, 0:AFTER, :]
    first_columns = edge[...].astype(BF16)
    even_ref[...] = jnp.where((me & 1) == 0, last_columns, first_columns)
    odd_ref[...] = jnp.where((me & 1) == 0, first_columns, last_columns)


def gather_four(shape):
    return (shape[0] + BEFORE[3] + AFTER) * shape[1]


def gather_three(shape):
    total = (shape[0] + BEFORE[2] + AFTER) * shape[1]
    return total, up_to(-(-total // 2), 8)


def own_channels(me, channels, own):
    return onehot(iota((channels, own), 0) == iota((channels, own), 1) + me * own)


def own_bias(line, first, me, own, count):
    total = None
    for j in range(count):
        part = jnp.where(me == j, line[0:1, first + j * own : first + (j + 1) * own], 0.0)
        total = part if total is None else total + part
    return total


def spread(target, blocks, me, rows, block_cols):
    shift = block_cols.bit_length() - 1
    width = target.shape[1]
    total = None
    for k, block in enumerate(blocks):
        size = block.shape[0]
        shape = (rows, width, size)
        source = iota(shape, 2)
        slot = (me ^ k) * block_cols + 1 + (source & (block_cols - 1))
        choose = ((source >> shift) == iota(shape, 0)) & (iota(shape, 1) == slot)
        part = dot(onehot(choose).reshape(rows * width, size), block)
        total = part if total is None else total + part
    target[...] = total.reshape(rows, width, total.shape[1])


def coarse_first_kernel(sizes, *refs):
    count, rows_all, high3, wide3, chan3, high4, wide4, chan4, bias3, bias4 = sizes
    blocks = refs[:count]
    conv3, conv4, bias_ref, _, out, res3, res4, full3, full4, message, line = refs[count:]
    row, me = position()
    bias_row(bias_ref, line)
    size4 = gather_four((high4, wide4))
    total3, head = gather_three((high3, wide3))
    spread(full4, [b[0:size4, 0:chan4] for b in blocks], me, high4 + BEFORE[3] + AFTER, wide4)
    parts = []
    for b in blocks:
        parts.append(
            jnp.concatenate(
                [
                    b[size4 : size4 + head, 0:chan3].astype(F32),
                    b[size4 : size4 + total3 - head, chan3 : 2 * chan3].astype(F32),
                ],
                axis=0,
            )
        )
    spread(full3, parts, me, high3 + BEFORE[2] + AFTER, wide3)
    heights = []
    for full, kernel, high, wide, chan, before, base in (
        (full3, conv3, high3, wide3, chan3, BEFORE[2], bias3),
        (full4, conv4, high4, wide4, chan4, BEFORE[3], bias4),
    ):
        own = chan // count
        out_high = high + before + AFTER - 2
        out_wide = wide * count
        mid = conv(full, out_high, out_wide, 0, 0, third(kernel, 0, own, 0, chan))
        mid = jax.nn.relu(mid + own_bias(line, base, me, own, count)).reshape(out_high, out_wide, own)
        rows = iota(mid.shape, 0) + row * high - (before - 1)
        valid = (rows >= 0) & (rows < rows_all * high)
        heights.append(jnp.where(valid, mid, 0.0).reshape(out_high * out_wide, own))
    mid3, mid4 = heights
    half = mid3.shape[0] // 2
    own3, own4 = mid3.shape[1], mid4.shape[1]
    message[0:half, 0:own3] = mid3[0:half]
    message[0:half, 64 : 64 + own3] = mid3[half:]
    message[half : half + mid4.shape[0], 0:own4] = mid4
    out[...] = message[...].astype(BF16)
    skip3 = BEFORE[2] - 1
    keep = full3[skip3 : skip3 + high3 + 1, 1 : 1 + wide3 * count, :].reshape(-1, chan3)
    res3[...] = dot(keep, own_channels(me, chan3, own3)).astype(BF16)
    keep = full4[BEFORE[3] : BEFORE[3] + high4, 1 : 1 + wide4 * count, :].reshape(-1, chan4)
    res4[...] = dot(keep, own_channels(me, chan4, own4)).astype(BF16)


def natural(blocks, me, own, channels):
    total = None
    for k, block in enumerate(blocks):
        place = onehot(iota((own, channels), 1) == iota((own, channels), 0) + (me ^ k) * own)
        part = dot(block, place)
        total = part if total is None else total + part
    return total


def message_rows(sizes):
    count, _, high3, wide3, _, high4, wide4, _, _, _ = sizes
    half = (high3 + BEFORE[2] + AFTER - 2) * wide3 * count // 2
    return half, half + (high4 + BEFORE[3] + AFTER - 2) * wide4 * count


def coarse_second_kernel(sizes, *refs):
    count, rows_all, high3, wide3, chan3, high4, wide4, chan4, bias3, bias4 = sizes
    blocks = refs[:count]
    res3, res4, conv3, conv4, bias_ref, _ = refs[count : count + 6]
    outs = refs[count + 6 : 2 * count + 6]
    full3, full4, message, line = refs[2 * count + 6 :]
    row, me = position()
    bias_row(bias_ref, line)
    own3, own4 = chan3 // count, chan4 // count
    half, last = message_rows(sizes)
    mids3 = [
        jnp.concatenate([b[0:half, 0:own3].astype(F32), b[0:half, 64 : 64 + own3].astype(F32)], axis=0)
        for b in blocks
    ]
    mids4 = [b[half:last, 0:own4] for b in blocks]
    results = []
    for full, mids, kernel, res, high, wide, chan, before, base, extra in (
        (full3, mids3, conv3, res3, high3, wide3, chan3, BEFORE[2], bias3, 1),
        (full4, mids4, conv4, res4, high4, wide4, chan4, BEFORE[3], bias4, 0),
    ):
        own = chan // count
        mid_high = high + before + AFTER - 2
        out_wide = wide * count
        full[...] = jnp.zeros_like(full)
        full[:, 1 : 1 + out_wide, :] = natural(mids, me, own, chan).reshape(mid_high, out_wide, chan)
        out_high = high + extra
        first = 9 * chan
        y = conv(full, out_high, out_wide, 0, 0, third(kernel, 0, own, first, chan))
        y = y + own_bias(line, base + chan, me, own, count) + res[...].astype(F32)
        y = jax.nn.relu(y).reshape(out_high, out_wide, own)
        rows = iota(y.shape, 0) + row * high - extra
        y = jnp.where((rows >= 0) & (rows < rows_all * high), y, 0.0)
        results.append(y.reshape(out_high * out_wide, own))
    y3, y4 = results
    for k, out in enumerate(outs):
        target = me ^ k
        wide = wide3 * count
        shape = (high3 + 1, 16, y3.shape[0])
        source = iota(shape, 2)
        slot = iota(shape, 1)
        choose = (
            ((source >> (wide.bit_length() - 1)) == iota(shape, 0))
            & ((source & (wide - 1)) == target * wide3 - 1 + slot)
            & (slot < wide3 + 1)
        )
        part = dot(onehot(choose).reshape((high3 + 1) * 16, -1), y3)
        cut = part.shape[0] // 2
        message[0:cut, 0:own3] = part[0:cut]
        message[0:cut, 64 : 64 + own3] = part[cut:]
        wide = wide4 * count
        shape = (high4, 8, y4.shape[0])
        source = iota(shape, 2)
        slot = iota(shape, 1)
        choose = (
            ((source >> (wide.bit_length() - 1)) == iota(shape, 0))
            & ((source & (wide - 1)) == target * wide4 + slot)
            & (slot < wide4)
        )
        part = dot(onehot(choose).reshape(high4 * 8, -1), y4)
        message[cut : cut + high4 * 8, 0:own4] = part
        out[...] = message[...].astype(BF16)


class Packing:
    def __init__(self, shapes):
        self.place = {}
        at = 0
        for name, (rows, width) in shapes.items():
            pad = up_to(width, 16)
            self.place[name] = (at, pad, width, rows)
            at += pad * -(-rows // LANES)
        self.total = at

    def tiles(self, name):
        at, pad, width, rows = self.place[name]
        for low in range(0, rows, LANES):
            yield at + low // LANES * pad, width, low, min(LANES, rows - low)

    def span(self, names):
        ends = [(self.place[n][0], self.place[n][0] + self.place[n][1] * -(-self.place[n][3] // LANES)) for n in names]
        return min(e[0] for e in ends), max(e[1] for e in ends)

    def scratch(self, name, count):
        _, _, width, rows = self.place[name]
        return pltpu.VMEM((width * count, rows), BF16 if width % 16 == 0 else F32)

    def unpack(self, name, stacked, base, target):
        for j in range(stacked.shape[0]):
            for at, width, low, size in self.tiles(name):
                target[j * width : (j + 1) * width, low : low + size] = stacked[
                    j, at - base : at - base + width, 0:size
                ].astype(target.dtype)


def pack_kernel(packings, *refs):
    inputs = sum(len(p.place) for p in packings)
    sources, outs = iter(refs[:inputs]), refs[inputs + 1 :]
    for packing, out in zip(packings, outs):
        for name in packing.place:
            source = next(sources)
            for at, width, low, size in packing.tiles(name):
                out[at : at + width, 0:size] = source[:, low : low + size]


def fetch(span, me, buffers, stacked, semaphores):
    copies = []
    for k, buffer in enumerate(buffers):
        copy = pltpu.make_async_copy(
            buffer.at[pl.ds(span[0], span[1] - span[0])], stacked.at[me ^ k], semaphores.at[k]
        )
        copy.start()
        copies.append(copy)
    return copies


def fine_kernel(plan, *refs):
    packing, layouts, count, rows_all, unit = plan
    one, two, rows_even, rows_odd, cols_even, cols_odd, bias_ref, _ = refs[:8]
    buffers = refs[8 : 8 + count]
    y1_ref, y2_ref, v1, v2 = refs[8 + count : 12 + count]
    x1, m1, x2, m2, k1, k2, stacked, line, semaphores = refs[12 + count :]
    row, me = position()
    span = packing.span(("conv_one", "conv_two"))
    copies = fetch(span, me, buffers, stacked, semaphores)
    rows_border, cols_border = Border(rows_even, rows_odd, row), Border(cols_even, cols_odd, me)
    bias_row(bias_ref, line)
    high1, wide1, chan1 = one.shape
    high2, wide2, chan2 = two.shape
    stretch_fine(0, layouts, one, rows_border, x1, 16)
    stretch_fine(1, layouts, two, rows_border, x2, 16)
    b1, b2 = BEFORE[0], BEFORE[1]
    rows2 = high2 + b2 + AFTER
    every = slice(None)
    x1[:, 16 - b1 : 16, :] = cols_border.prev(every, slice(0, b1), slice(0, chan1))
    x1[:, 16 + wide1 : 16 + wide1 + AFTER, :] = cols_border.next(every, slice(0, AFTER), slice(0, chan1))
    x2[:, 16 - b2 : 16, :] = cols_border.prev(slice(0, rows2), slice(b1, b1 + b2), slice(0, chan2))
    x2[:, 16 + wide2 : 16 + wide2 + AFTER, :] = cols_border.next(
        slice(0, rows2), slice(AFTER, 2 * AFTER), slice(0, chan2)
    )
    for copy in copies:
        copy.wait()
    packing.unpack("conv_one", stacked, 0, k1)
    packing.unpack("conv_two", stacked, 0, k2)
    ys = []
    for x, m, v, k, before, high, wide, chan, base in (
        (x1, m1, v1, k1, b1, high1, wide1, chan1, 0),
        (x2, m2, v2, k2, b2, high2, wide2, chan2, 2 * unit),
    ):
        mid_high = high + before
        mid_wide = up_to(wide + before, 16)
        mid = conv(x, mid_high, mid_wide, 0, 16 - before, third(k, 0, chan, 0, chan))
        mid = jax.nn.relu(mid + line[0:1, base : base + chan]).reshape(mid_high, mid_wide, chan)
        ok = inside(
            mid.shape, row * high - before + 1, rows_all * high, me * wide - before + 1, count * wide
        )
        m[:, 0:mid_wide, :] = rounded(jnp.where(ok, mid, 0.0))
        y_high = high + before - 2
        y_wide = up_to(wide + before - 2, 16)
        y = conv(m, y_high, y_wide, 0, 0, third(k, 0, chan, 9 * chan, chan))
        y = y + line[0:1, base + chan : base + 2 * chan]
        y = y.reshape(y_high, y_wide, chan) + x[2 : 2 + y_high, 18 - before : 18 - before + y_wide, :]
        skip = before - 2
        ok = inside(y.shape, row * high - skip, rows_all * high, me * wide - skip, count * wide)
        v[:, 0:y_wide, 0:chan] = rounded(jnp.where(ok, jax.nn.relu(y), 0.0))
        ys.append(v[skip : skip + high, skip : skip + wide, 0:chan].astype(BF16))
    y1_ref[...] = ys[0]
    y2_ref[...] = ys[1]


def down_kernel(plan, *refs):
    packings, count, rows_all, unit, offs, shapes = plan
    v1, v2, bias_ref, _ = refs[:4]
    buffers = (refs[4 : 4 + count], refs[4 + count : 4 + 2 * count])
    d12_ref, d3_ref, d4_ref = refs[4 + 2 * count : 7 + 2 * count]
    t1, tb, s12, t2, s3, g1, g2, stacked1, stacked2, line, semaphores1, semaphores2 = refs[7 + 2 * count :]
    row, me = position()
    spans = packings[0].span(("down_one",)), packings[1].span(("down_two",))
    copies = fetch(spans[0], me, buffers[0], stacked1, semaphores1)
    copies += fetch(spans[1], me, buffers[1], stacked2, semaphores2)
    bias_row(bias_ref, line)
    for copy in copies:
        copy.wait()
    packings[0].unpack("down_one", stacked1, spans[0][0], g1)
    packings[1].unpack("down_two", stacked2, spans[1][0], g2)
    (high1, wide1, _), (_, _, chan2) = shapes[:2]
    off1, off2 = offs[0], offs[1]
    half_high, half_wide = high1 // 2, wide1 // 2
    out_high, out_wide = half_high + 3, up_to(half_wide + 3, 8)
    first = conv_strided((v1,), out_high, out_wide, 0, 0, (0, unit), third(g1, 0, 4 * unit, 0, unit))
    first = first + line[0:1, off1 : off1 + 4 * unit]
    s12[...] = first[:, 0 : 2 * unit].reshape(out_high, out_wide, 2 * unit)
    d12_ref[...] = s12[3 : 3 + half_high, 3 : 3 + half_wide, :]
    t = jax.nn.relu(first[:, 2 * unit : 4 * unit]).reshape(out_high, out_wide, 2 * unit)
    ok = inside(t.shape, row * half_high - 3, rows_all * half_high, me * half_wide - 3, count * half_wide)
    t1[:, 0:out_wide, 0 : 2 * unit] = rounded(jnp.where(ok, t, 0.0))
    quarter_high, quarter_wide = half_high // 2, half_wide // 2
    d13 = conv_strided(
        (t1,), quarter_high, quarter_wide, 2, 2, (0, unit), third(g1, 4 * unit, 8 * unit, 0, unit)
    )
    d13 = d13 + line[0:1, off1 + 4 * unit : off1 + 8 * unit]
    q_high, q_wide = quarter_high + 1, up_to(quarter_wide + 1, 8)
    t14b = conv_strided((t1,), q_high, q_wide, 0, 0, (unit, 2 * unit), third(g1, 8 * unit, 9 * unit, 0, unit))
    t14b = jax.nn.relu(t14b + line[0:1, off1 + 8 * unit : off1 + 9 * unit]).reshape(q_high, q_wide, unit)
    q_args = (row * quarter_high - 1, rows_all * quarter_high, me * quarter_wide - 1, count * quarter_wide)
    tb[:, 0:q_wide, 0:unit] = rounded(jnp.where(inside(t14b.shape, *q_args), t14b, 0.0))
    e_high, e_wide = quarter_high // 2, 8
    d14 = conv_strided((tb,), e_high, e_wide, 0, 0, (0, unit), third(g1, 9 * unit, 17 * unit, 0, unit))
    d14 = d14 + line[0:1, off1 + 9 * unit : off1 + 17 * unit]
    second = conv_strided((v2,), q_high, q_wide, 0, 0, (0, chan2), third(g2, 0, 6 * unit, 0, chan2))
    second = second + line[0:1, off2 : off2 + 6 * unit]
    s3[...] = second[:, 0 : 4 * unit].reshape(q_high, q_wide, 4 * unit)
    d3_ref[...] = d13.reshape(quarter_high, quarter_wide, 4 * unit) + s3[
        1 : 1 + quarter_high, 1 : 1 + quarter_wide, :
    ]
    t24 = jax.nn.relu(second[:, 4 * unit : 6 * unit]).reshape(q_high, q_wide, 2 * unit)
    t2[:, 0:q_wide, 0 : 2 * unit] = rounded(jnp.where(inside(t24.shape, *q_args), t24, 0.0))
    d24 = conv_strided((t2,), e_high, e_wide, 0, 0, (0, 2 * unit), third(g2, 6 * unit, 14 * unit, 0, chan2))
    d24 = d24 + line[0:1, off2 + 6 * unit : off2 + 14 * unit]
    d4_ref[...] = (d14 + d24).reshape(e_high, e_wide, 8 * unit)


LIFTS = ("lift_two", "lift_three", "lift_four")


def join_kernel(plan, *refs):
    packings, count, unit, offs, shapes = plan
    blocks = refs[:count]
    y1_ref, y2_ref, d12_ref, d3_ref, d4_ref, bias_ref = refs[count : count + 6]
    buffers = refs[count + 6 : 2 * count + 6], refs[2 * count + 6 : 3 * count + 6]
    out1, out2, out3, out4 = refs[3 * count + 6 : 3 * count + 10]
    (v3a, v3b, a2, a3a, a3b, a1, p2, p1, c3, l2, l3, l4, k3, stacked1, stacked2, line, semaphores1, semaphores2) = refs[3 * count + 10 :]
    _, me = position()
    spans = packings[0].span(LIFTS), packings[1].span(("down_three",))
    copies = fetch(spans[0], me, buffers[0], stacked1, semaphores1)
    copies += fetch(spans[1], me, buffers[1], stacked2, semaphores2)
    bias_row(bias_ref, line)
    (high2, wide2, chan2), (high3, wide3, chan3), (high4, wide4, chan4) = shapes[1:]
    own3, own4 = chan3 // count, chan4 // count
    cut = (high3 + 1) * 8
    parts = [
        jnp.concatenate([b[0:cut, 0:own3].astype(F32), b[0:cut, 64 : 64 + own3].astype(F32)], axis=0)
        for b in blocks
    ]
    whole3 = natural(parts, me, own3, chan3).reshape(high3 + 1, 16, chan3)
    v3 = (v3a, v3b)
    wide_store(v3, slice(None), slice(0, 16), whole3)
    y4 = natural([b[cut : cut + high4 * 8, 0:own4] for b in blocks], me, own4, chan4)
    y3 = wide_load(v3, slice(1, 1 + high3), slice(1, 1 + wide3))[:, :, 0:chan3]
    for copy in copies:
        copy.wait()
    groups3, groups4 = (unit, 2 * unit), (unit, 2 * unit, 4 * unit)
    for name, target in zip(LIFTS, (l2, l3, l4)):
        packings[0].unpack(name, stacked1, spans[0][0], target)
    packings[1].unpack("down_three", stacked2, spans[1][0], k3)
    off3, offl2, offl3, offl4 = offs[2:]

    def lifted(flat, kernel, groups, offset):
        values, first = [], 0
        for group in groups:
            value = dot_t(flat, kernel[first : first + group, :])
            values.append(value + line[0:1, offset + first : offset + first + group])
            first += group
        return values

    def double(scratch, value, keep):
        high, wide, channels = value.shape
        for r in range(2):
            for q in range(2):
                wide_store(scratch, pl.ds(r, high, stride=2), pl.ds(q, wide, stride=2), value)
        return wide_load(scratch, slice(0, 2 * high), slice(0, keep))[:, :, 0:channels]

    u4 = [u.reshape(high4, 8, -1) for u in lifted(y4, l4, groups4, offl4)]
    u3 = [u.reshape(high3, wide3, -1) for u in lifted(y3.reshape(high3 * wide3, chan3), l3, groups3, offl3)]
    y2 = y2_ref[...]
    (u2,) = lifted(y2.reshape(high2 * wide2, chan2), l2, (unit,), offl2)
    d34 = conv_strided(v3, high4, 8, 0, 0, (0, chan3), third(k3, 0, chan4, 0, chan3))
    d34 = d34 + line[0:1, off3 : off3 + chan4]
    four = jax.nn.relu(d4_ref[...] + (d34 + y4).reshape(high4, 8, chan4))
    c3[...] = four
    out4[...] = c3[:, 0:wide4, :].astype(BF16)
    three = double((a3a, a3b), u4[2], wide3) + d3_ref[...] + y3
    out3[...] = jax.nn.relu(three).astype(BF16)
    two = double((a2,), u4[1], wide3) + u3[1]
    two = double((p2,), two, wide2) + d12_ref[...] + y2.astype(F32)
    out2[...] = jax.nn.relu(two).astype(BF16)
    fine = double((a1,), u4[0], wide3) + u3[0]
    fine = double((p1,), fine, wide2) + u2.reshape(high2, wide2, unit)
    fine = double((p1,), fine, shapes[0][1]) + y1_ref[...].astype(F32)
    out1[...] = jax.nn.relu(fine).astype(BF16)


def offsets(width):
    start = 30 * width
    return (
        start,
        start + 17 * width,
        start + 31 * width,
        start + 39 * width,
        start + 40 * width,
        start + 43 * width,
    )


def flipped(value, mask, count):
    return lax.ppermute(value, "cols", [(i, i ^ mask) for i in range(count)])


def paired(even, odd, axis):
    count = lax.axis_size(axis)
    results = []
    for value, start in ((even, 0), (odd, 1)):
        ups = [(i, i + 1) for i in range(start, count - 1, 2)]
        results.append(lax.ppermute(value, axis, ups + [(b, a) for a, b in ups]))
    return results


def exchanged(value, count):
    return [value] + [flipped(value, mask, count) for mask in range(1, count)]


def gathered(value, count):
    held = {0: value}
    for b in range(1, count.bit_length() - 1):
        for mask in list(held):
            held[mask | 1 << b] = flipped(held[mask], 1 << b, count)
    if count > 1:
        for mask in list(held):
            held[mask | 1] = flipped(held[mask], 1, count)
    return [held[mask] for mask in range(count)]


def stack(packing, names, count):
    low, high = packing.span(names)
    return pltpu.VMEM((count, high - low, LANES), BF16)


def local(kernel, cost, outs, scratch, operands, anywhere=()):
    return pl.pallas_call(
        kernel,
        out_shape=list(outs),
        in_specs=vmem(len(operands)) + [pl.BlockSpec(memory_space=pl.ANY)] * len(anywhere),
        out_specs=vmem(len(outs)),
        scratch_shapes=scratch,
        compiler_params=PARAMS,
        cost_estimate=pl.CostEstimate(flops=int(cost * 1.15e9), bytes_accessed=0, transcendentals=0),
    )(*operands, *anywhere)


def on_device(
    feat_one,
    feat_two,
    feat_three,
    feat_four,
    conv_one,
    conv_two,
    conv_three,
    conv_four,
    down_one,
    down_two,
    down_three,
    lift_two,
    lift_three,
    lift_four,
    biases,
):
    count = lax.axis_size("cols")
    row_total = lax.axis_size("rows")
    feats = (feat_one, feat_two, feat_three, feat_four)
    shapes = tuple(f.shape for f in feats)
    unit = feat_one.shape[2]
    offs = offsets(unit)
    lines = biases.shape[0] // LANES
    bias = biases.reshape(lines, LANES)
    line = pltpu.VMEM((8, lines * LANES), F32)
    layouts = (RowLayout(shapes, BEFORE), RowLayout(shapes, (AFTER,) * 4))
    most = max(layouts[0].total, layouts[1].total)
    rows_pair = local(
        functools.partial(rows_kernel, layouts),
        1.5,
        [jax.ShapeDtypeStruct((most, LANES), BF16)] * 2,
        [pltpu.VMEM((most, LANES), F32)],
        feats,
    )
    rows_border = paired(*rows_pair, "rows")

    groups = (
        {"conv_one": conv_one, "conv_two": conv_two, "down_one": down_one},
        {"down_two": down_two, "lift_two": lift_two, "lift_three": lift_three, "lift_four": lift_four},
        {"down_three": down_three},
    )
    packings = [Packing({name: w.shape for name, w in group.items()}) for group in groups]
    packed = local(
        functools.partial(pack_kernel, packings),
        1.5,
        [jax.ShapeDtypeStruct((p.total, LANES), BF16) for p in packings],
        [],
        [w.T for group in groups for w in group.values()],
        [rows_pair[0]],
    )
    early_buffers = gathered(packed[0], count)
    middle_buffers = gathered(packed[1], count)
    late_buffers = gathered(packed[2], count)

    (high1, wide1, chan1), (high2, wide2, chan2), (high3, wide3, chan3), (high4, wide4, chan4) = shapes
    size4 = gather_four(shapes[3])
    total3, head3 = gather_three(shapes[2])
    lanes = max(chan4, 2 * chan3)
    rows1 = high1 + BEFORE[0] + AFTER
    rows2 = high2 + BEFORE[1] + AFTER
    (gather,) = local(
        functools.partial(columns_kernel, layouts),
        1.0,
        [jax.ShapeDtypeStruct((size4 + head3, lanes), BF16)],
        [pltpu.VMEM((total3, chan3), F32), pltpu.VMEM((size4 + head3, lanes), F32)],
        (feat_three, feat_four, *rows_border),
        [packed[1]],
    )
    coarse = exchanged(gather, count)
    cols_pair = local(
        functools.partial(edges_kernel, layouts),
        1.5,
        [jax.ShapeDtypeStruct((rows1, 16, LANES), BF16)] * 2,
        [
            pltpu.VMEM((rows1, wide1, chan1), F32),
            pltpu.VMEM((rows2, wide2, chan2), F32),
            pltpu.VMEM((rows1, 16, LANES), F32),
        ],
        (feat_one, feat_two, *rows_border),
        [gather],
    )
    cols_border = paired(*cols_pair, "cols")

    sizes = (count, row_total, high3, wide3, chan3, high4, wide4, chan4, 6 * unit, 14 * unit)
    own3, own4 = chan3 // count, chan4 // count
    _, last = message_rows(sizes)
    full_wide3, full_wide4 = up_to(wide3 * count + 2, 8), up_to(wide4 * count + 2, 8)
    three_t, four_t = conv_three.T, conv_four.T
    mid, res3, res4 = local(
        functools.partial(coarse_first_kernel, sizes),
        3.0,
        [
            jax.ShapeDtypeStruct((last, LANES), BF16),
            jax.ShapeDtypeStruct(((high3 + 1) * wide3 * count, own3), BF16),
            jax.ShapeDtypeStruct((high4 * wide4 * count, own4), BF16),
        ],
        [
            pltpu.VMEM((high3 + BEFORE[2] + AFTER, full_wide3, chan3), F32),
            pltpu.VMEM((high4 + BEFORE[3] + AFTER, full_wide4, chan4), F32),
            pltpu.VMEM((last, LANES), F32),
            line,
        ],
        (*coarse, three_t, four_t, bias),
        [cols_pair[0]],
    )
    mids = exchanged(mid, count)

    mid_wide1, mid_wide2 = up_to(wide1 + BEFORE[0], 16), up_to(wide2 + BEFORE[1], 16)
    y_wide1, y_wide2 = up_to(wide1 + BEFORE[0] - 2, 16), up_to(wide2 + BEFORE[1] - 2, 16)
    half_wide = up_to(wide1 // 2 + 3, 8)
    quarter_wide = up_to(wide1 // 4 + 1, 8)
    y1, y2, v1, v2 = local(
        functools.partial(fine_kernel, (packings[0], layouts, count, row_total, unit)),
        5.0,
        [
            jax.ShapeDtypeStruct(shapes[0], BF16),
            jax.ShapeDtypeStruct(shapes[1], BF16),
            jax.ShapeDtypeStruct((high1 + BEFORE[0] - 2, max(2 * half_wide, y_wide1) + 8, LANES), F32),
            jax.ShapeDtypeStruct((high2 + BEFORE[1] - 2, max(2 * quarter_wide, y_wide2) + 8, LANES), F32),
        ],
        [
            pltpu.VMEM((rows1, 24 + mid_wide1, chan1), F32),
            pltpu.VMEM((high1 + BEFORE[0], max(mid_wide1, y_wide1) + 8, chan1), F32),
            pltpu.VMEM((rows2, 24 + mid_wide2, chan2), F32),
            pltpu.VMEM((high2 + BEFORE[1], max(mid_wide2, y_wide2) + 8, chan2), F32),
            packings[0].scratch("conv_one", count),
            packings[0].scratch("conv_two", count),
            stack(packings[0], ("conv_one", "conv_two"), count),
            line,
            pltpu.SemaphoreType.DMA((count,)),
        ],
        (feat_one, feat_two, *rows_border, *cols_border, bias),
        [mid, *early_buffers],
    )

    message = (high3 + 1) * 8 + high4 * 8
    sent = local(
        functools.partial(coarse_second_kernel, sizes),
        3.0,
        [jax.ShapeDtypeStruct((message, LANES), BF16)] * count,
        [
            pltpu.VMEM((high3 + BEFORE[2] + AFTER - 2, full_wide3, chan3), F32),
            pltpu.VMEM((high4 + BEFORE[3] + AFTER - 2, full_wide4, chan4), F32),
            pltpu.VMEM((message, LANES), F32),
            line,
        ],
        (*mids, res3, res4, three_t, four_t, bias),
        [y1],
    )
    coarse_out = [sent[0]] + [flipped(sent[mask], mask, count) for mask in range(1, count)]

    downs = local(
        functools.partial(down_kernel, (packings[:2], count, row_total, unit, offs, shapes)),
        5.0,
        [
            jax.ShapeDtypeStruct((high1 // 2, wide1 // 2, 2 * unit), F32),
            jax.ShapeDtypeStruct((high1 // 4, wide1 // 4, 4 * unit), F32),
            jax.ShapeDtypeStruct((high1 // 8, 8, 8 * unit), F32),
        ],
        [
            pltpu.VMEM((high1 // 2 + 3, max(2 * quarter_wide, half_wide) + 8, LANES), F32),
            pltpu.VMEM((high1 // 4 + 1, max(16, quarter_wide) + 8, LANES), F32),
            pltpu.VMEM((high1 // 2 + 3, half_wide, 2 * unit), F32),
            pltpu.VMEM((high1 // 4 + 1, max(16, quarter_wide) + 8, LANES), F32),
            pltpu.VMEM((high1 // 4 + 1, quarter_wide, 4 * unit), F32),
            packings[0].scratch("down_one", count),
            packings[1].scratch("down_two", count),
            stack(packings[0], ("down_one",), count),
            stack(packings[1], ("down_two",), count),
            line,
            pltpu.SemaphoreType.DMA((count,)),
            pltpu.SemaphoreType.DMA((count,)),
        ],
        (v1, v2, bias),
        [sent[0], *early_buffers, *middle_buffers],
    )

    return tuple(
        local(
            functools.partial(join_kernel, (packings[1:], count, unit, offs, shapes)),
            4.0,
            [jax.ShapeDtypeStruct(shape, BF16) for shape in shapes],
            [
                pltpu.VMEM((high3 + 1, 24, LANES), F32),
                pltpu.VMEM((high3 + 1, 24, LANES), F32),
                pltpu.VMEM((2 * high4, 16, LANES), F32),
                pltpu.VMEM((2 * high4, 16, LANES), F32),
                pltpu.VMEM((2 * high4, 16, LANES), F32),
                pltpu.VMEM((2 * high4, 16, LANES), F32),
                pltpu.VMEM((high2, wide2, LANES), F32),
                pltpu.VMEM((high1, wide1, LANES), F32),
                pltpu.VMEM((high4, 8, chan4), F32),
                *[packings[1].scratch(name, count) for name in LIFTS],
                packings[2].scratch("down_three", count),
                stack(packings[1], LIFTS, count),
                stack(packings[2], ("down_three",), count),
                line,
                pltpu.SemaphoreType.DMA((count,)),
                pltpu.SemaphoreType.DMA((count,)),
            ],
            (*coarse_out, y1, y2, *downs, bias),
            [*middle_buffers, *late_buffers],
        )
    )


def solution(mesh):
    spatial = P(("win", "rows"), "cols", None)
    placed = (spatial,) * 4 + (P(None, "cols"),) * 10 + (P(),)
    return jax.shard_map(
        on_device,
        mesh=mesh,
        in_specs=placed,
        out_specs=(spatial,) * 4,
        check_vma=False,
    )
```
